512 devices in a mesh: bins: 32 (over z, core), nuis: 16 (over y, x).
Axes of the slice: x: 4, y: 4, z: 16, core: 2. Of those that a mesh axis runs over, the one named last changes fastest.
Arguments:
- log_nominal: float32 [8192, 8], P('bins'), may hold values from -1 to 3
- variations: bfloat16 [8192, 8, 2048], P('bins', None, 'nuis'), may hold values from -0.0625 to 0.0625
- observed: int32 [8192], P('bins'), may hold values from 0 to 95
- start: float32 [2048], P('nuis'), may hold values from -5 to 5
- direction: float32 [2048], P('nuis'), may hold values from -5 to 5
- step_lengths: float32 [3], replicated, may hold values from 0.05 to 0.6
Outputs:
- line_change: float32 [3], replicated
- gradient: float32 [2048], P('nuis')
- hessian: float32 [2048, 2048], P('bins', 'nuis')
The draws below stay inside these ranges and needn't reach their ends.
All inputs are finite; a program needn't handle non-finite values.
Results may differ from the reference program's by a relative error of at most 0.022.
Values may be sent and summed in bfloat16 or wider, within the bound.
No kernel may reach another device: no remote copies, remote signals or barrier semaphores. Data moves between devices by JAX's collectives and lax.ppermute only.
A program may use at most 64 MiB of HBM per device.

```python
import jax
import jax.numpy as jnp
from jax import lax

P_SIZE = 8
K = 2048
BIN_DEV = 256
BINS = 8192


def set_ends(drawn, own_key, smallest, high):
    place = [jax.random.randint(jax.random.fold_in(own_key, axis), (), 0, length) for axis, length in enumerate(drawn.shape)]
    longest = drawn.shape.index(max(drawn.shape))
    beside = place[:longest] + [(place[longest] + 1) % drawn.shape[longest]] + place[longest + 1:]
    return drawn.at[tuple(place)].set(smallest).at[tuple(beside)].set(high)


def block_levels(rng, shape, split, smallest, top_value):
    def one(axis_at, parts):
        heights = jax.random.uniform(jax.random.fold_in(jax.random.fold_in(rng, 6), axis_at), (parts,), jnp.float32, smallest / len(split), top_value / len(split))
        return jnp.repeat(jnp.exp(heights), shape[axis_at] // parts).reshape((-1,) + (1,) * (len(shape) - axis_at - 1))

    gain = one(*split[0])
    for cut in split[1:]:
        gain = gain * one(*cut)
    return gain


def noise(rng, extent, width, bound, pieces=(), held_as=jnp.bfloat16):
    array = jax.random.normal(rng, extent, jnp.float32) * width
    if len(pieces) > 0:
        array = block_levels(rng, extent, pieces, -0.22, 0.18) * array
    return jnp.clip(array, min=-bound, max=bound).astype(held_as)


def setup_inputs(seed: int = 0) -> dict:
    key_of = jax.random.split(jax.random.key(seed), 7)
    return {
        "log_nominal": jnp.clip(-1.0 + 4.0 * jax.random.uniform(key_of[0], (BINS, P_SIZE), jnp.float32) ** block_levels(key_of[0], (BINS, P_SIZE), ((0, 32),), -0.2, 0.2), -1.0, 3.0),
        "variations": noise(key_of[1], (BINS, P_SIZE, K), (4 * K) ** -0.5, 0.0625, ((0, 32), (2, 16))),
        "observed": set_ends(jax.random.randint(key_of[2], (BINS,), 0, 96), jax.random.fold_in(key_of[2], 1), 0, 95).astype(jnp.int32),
        "start": noise(key_of[3], (K,), 1.0, 5.0, ((0, 16),), jnp.float32),
        "direction": noise(key_of[4], (K,), 1.0, 5.0, ((0, 16),), jnp.float32),
        "step_lengths": jnp.clip(jax.random.uniform(key_of[5], (3,), jnp.float32, 0.05, 0.6), 0.05, 0.6),
    }


def reference(log_nominal, variations, observed, start, direction, step_lengths):
    bin_total = observed.shape[0]
    proc_count = log_nominal.shape[1]
    full_width = start.shape[0]
    points = start[None, :] + step_lengths[:, None] * direction[None, :]
    all_points = jnp.concatenate([start[None, :], points], 0)
    step_count = bin_total // BIN_DEV

    def accumulate(state_in, step_index):
        hess_sum, grad_sum, change = state_in
        offset = (step_index * BIN_DEV).astype(jnp.int32)
        var_block = lax.dynamic_slice_in_dim(variations, offset, BIN_DEV, 0)
        nominal = lax.dynamic_slice_in_dim(log_nominal, offset, BIN_DEV, 0)
        counts = lax.dynamic_slice_in_dim(observed, offset, BIN_DEV, 0).astype(jnp.float32)
        var_rows = var_block.reshape(BIN_DEV * proc_count, full_width).astype(jnp.float32)
        shifts = jnp.dot(var_rows, all_points.T, precision=lax.Precision.HIGHEST).reshape(BIN_DEV, proc_count, 4)
        yields = jnp.exp(nominal[:, :, None] + shifts)
        expected = jnp.sum(yields, axis=1)
        log_expected = jnp.log(expected)
        change_rows = (expected[:, 1:] - expected[:, :1]) - counts[:, None] * (log_expected[:, 1:] - log_expected[:, :1])
        change = change + jnp.sum(change_rows, axis=0)
        base_yield = yields[:, :, 0]
        base_total = expected[:, 0]
        var_float = var_block.astype(jnp.float32)
        jacobian = jnp.sum(base_yield[:, :, None] * var_float, axis=1)
        residual = 1.0 - counts / base_total
        grad_sum = grad_sum + jnp.sum(residual[:, None] * jacobian, axis=0)
        left_var = ((residual[:, None] * base_yield)[:, :, None] * var_float).astype(jnp.bfloat16)
        left_var = left_var.reshape(BIN_DEV * proc_count, full_width).astype(jnp.float32)
        left_jac = ((counts / (base_total * base_total))[:, None] * jacobian).astype(jnp.bfloat16).astype(jnp.float32)
        right_jac = jacobian.astype(jnp.bfloat16).astype(jnp.float32)
        hess_sum = hess_sum + jnp.dot(var_rows.T, left_var, precision=lax.Precision.HIGHEST)
        hess_sum = hess_sum + jnp.dot(right_jac.T, left_jac, precision=lax.Precision.HIGHEST)
        return (hess_sum, grad_sum, change), None

    initial = (jnp.zeros((full_width, full_width), jnp.float32), jnp.zeros((full_width,), jnp.float32), jnp.zeros((3,), jnp.float32))
    final, unused = lax.scan(accumulate, initial, jnp.arange(step_count, dtype=jnp.int32))
    hess_sum, grad_sum, change = final
    squares = jnp.sum(all_points * all_points, axis=1)
    line_change = (change + 0.5 * (squares[1:] - squares[0])) / bin_total
    gradient = (grad_sum + start) / bin_total
    hessian = (hess_sum + jnp.eye(full_width, dtype=jnp.float32)) / bin_total
    return line_change, gradient, hessian
```

```python
import jax
import jax.numpy as jnp
import numpy as np
from jax import lax
from jax.experimental import pallas as pl
from jax.experimental.pallas import tpu as pltpu
from jax.sharding import Mesh
from jax.sharding import PartitionSpec as P


F32 = jnp.float32
BF16 = jnp.bfloat16
SIDE = 4
PROC = 8
ROWS = 2048
BINS_DEV = 256
LANES = 128
CHUNKS = ROWS // LANES
DEPTH = ROWS + BINS_DEV
VMEM = pl.BlockSpec(memory_space=pltpu.VMEM)
SMEM = pl.BlockSpec(memory_space=pltpu.SMEM)
PARAMS = pltpu.CompilerParams(vmem_limit_bytes=48 * 1024 * 1024)


def cost(flops, moved):
    return pl.CostEstimate(flops=flops, bytes_accessed=moved, transcendentals=0)


def thirds(x):
    high = x.astype(BF16)
    rest = x - high.astype(F32)
    middle = rest.astype(BF16)
    low = (rest - middle.astype(F32)).astype(BF16)
    return [high, middle, low]


def rows_dot(a, b):
    return lax.dot_general(a, b, (((1,), (0,)), ((), ())), preferred_element_type=F32)


def project_kernel(v_ref, start_ref, dir_ref, steps_ref, out_ref, flat):
    start, direction = start_ref[...], dir_ref[...]
    parts = jnp.concatenate(thirds(start) + thirds(direction), 0)
    six = lax.dot_general(
        parts, v_ref[...], (((1,), (1,)), ((), ())), preferred_element_type=F32
    )
    along_start = six[0:1] + six[1:2] + six[2:3]
    along_dir = six[3:4] + six[4:5] + six[5:6]
    for c in range(CHUNKS):
        span = slice(c * LANES, (c + 1) * LANES)
        flat[c : c + 1, :] = along_start[:, span]
        flat[CHUNKS + c : CHUNKS + c + 1, :] = along_dir[:, span]
    flat[2 * CHUNKS : 2 * CHUNKS + 8, :] = jnp.zeros((8, LANES), F32)
    flat[2 * CHUNKS : 2 * CHUNKS + 1, :] = start * start
    for j in range(3):
        point = start + steps_ref[j] * direction
        flat[2 * CHUNKS + 1 + j : 2 * CHUNKS + 2 + j, :] = point * point
    whole = flat[...]
    for i in range(out_ref.shape[0]):
        out_ref[i] = whole


def lane_groups_sum(x, lane):
    for k in (1, 2, 4):
        up = pltpu.roll(x, k, 1)
        down = pltpu.roll(x, LANES - k, 1)
        x = x + jnp.where((lane & k) != 0, up, down)
    return x


def weights_kernel(got_ref, nominal_ref, counts_ref, steps_ref, v_ref, w_ref, bins_ref, sq_ref):
    total = jnp.sum(got_ref[...], axis=0)
    along_start = total[0:CHUNKS]
    along_dir = total[CHUNKS : 2 * CHUNKS]
    sq_ref[...] = total[2 * CHUNKS : 2 * CHUNKS + 8]
    nominal, counts = nominal_ref[...], counts_ref[...]
    lane = lax.broadcasted_iota(jnp.int32, (CHUNKS, LANES), 1)
    base = jnp.exp(nominal + along_start)
    base_total = lane_groups_sum(base, lane)
    base_log = jnp.log(base_total)
    part = [None] * 3
    for j in range(3):
        shifted = jnp.exp(nominal + (along_start + steps_ref[j] * along_dir))
        expected = lane_groups_sum(shifted, lane)
        change = (expected - base_total) - counts * (jnp.log(expected) - base_log)
        part[j] = jnp.sum(change, axis=0, keepdims=True) * (1.0 / PROC)
    residual = 1.0 - counts / base_total
    left = residual * base
    w_ref[0] = base
    w_ref[1] = left
    w_ref[2] = (counts / (base_total * base_total)) * base
    grad = jnp.zeros((3, LANES), F32)
    for c in range(CHUNKS):
        row = jnp.concatenate(thirds(left[c : c + 1]), 0)
        grad = grad + rows_dot(row, v_ref[c * LANES : (c + 1) * LANES, :])
    grad = jnp.sum(grad, axis=0, keepdims=True)
    tile = jnp.concatenate([grad] + part + [jnp.zeros((4, LANES), F32)], 0)
    for i in range(bins_ref.shape[0]):
        bins_ref[i] = tile


def hessian_kernel(pos_ref, w_ref, own, x1, x3, x2, y1, y3, y2, out_ref, rights, lefts):
    px, py = pos_ref[0], pos_ref[1]
    mine = lax.broadcasted_iota(jnp.int32, (16, LANES), 1) // PROC
    mine = mine == lax.broadcasted_iota(jnp.int32, (16, LANES), 0)
    columns = w_ref[1].T
    for c in range(CHUNKS):
        span = slice(c * LANES, (c + 1) * LANES)
        jac_span = slice(ROWS + c * 16, ROWS + (c + 1) * 16)
        both = []
        for k in (0, 2):
            spread = jnp.where(mine, w_ref[k, c : c + 1, :], 0.0)
            both.append(jnp.concatenate(thirds(spread), 0))
        scale = columns[:, c : c + 1]
        for step, ref in enumerate((own, x1, x2, x3)):
            at = lax.rem(px + step, SIDE)
            rows = ref[span, :]
            rights[at, span, :] = rows
            jac = rows_dot(both[0], rows)
            rights[at, jac_span, :] = (jac[0:16] + jac[16:32] + jac[32:48]).astype(BF16)
        for step, ref in enumerate((own, y1, y2, y3)):
            at = lax.rem(py + step, SIDE)
            rows = ref[span, :]
            lefts[at, span, :] = (scale * rows.astype(F32)).astype(BF16)
            jac = rows_dot(both[1], rows)
            lefts[at, jac_span, :] = (jac[0:16] + jac[16:32] + jac[32:48]).astype(BF16)
    right = jnp.concatenate([rights[k] for k in range(SIDE)], 1)
    for j in range(SIDE):
        term = lax.dot_general(
            right, lefts[j], (((0,), (0,)), ((), ())), preferred_element_type=F32
        ).astype(BF16)
        for i in range(SIDE):
            for half in range(2):
                at = i * LANES + half * 64
                out_ref[half, j, i] = term[at : at + 64]


def arrays_of(*shapes):
    return tuple(jax.ShapeDtypeStruct(s, d) for s, d in shapes)


def from_ahead(array, axis, step):
    return lax.ppermute(array, axis, [((i + step) % SIDE, i) for i in range(SIDE)])


def exchanged(array, axes):
    return lax.all_to_all(array, axes, 0, 0, tiled=True)


def shards(log_nominal, variations, observed, start, direction, step_lengths):
    bin_total = 32 * BINS_DEV
    own = variations.reshape(ROWS, LANES)
    x1, x3, x2 = (from_ahead(own, "x", k) for k in (1, 3, 2))
    y1, y3, y2 = (from_ahead(own, "y", k) for k in (1, 3, 2))
    sent = pl.pallas_call(
        project_kernel,
        out_shape=jax.ShapeDtypeStruct((16, 40, LANES), F32),
        in_specs=[VMEM, VMEM, VMEM, SMEM],
        out_specs=VMEM,
        scratch_shapes=[pltpu.VMEM((40, LANES), F32)],
        compiler_params=PARAMS,
        cost_estimate=cost(10_000_000, 1_000_000),
        name="project",
    )(own, start[None, :], direction[None, :], step_lengths)
    got = exchanged(sent, ("y", "x"))
    nominal = log_nominal.reshape(CHUNKS, LANES)
    counts = jnp.repeat(observed.astype(F32), PROC).reshape(CHUNKS, LANES)
    weights, bins_part, squares = pl.pallas_call(
        weights_kernel,
        out_shape=arrays_of(
            ((3, CHUNKS, LANES), F32), ((32, 8, LANES), F32), ((8, LANES), F32)
        ),
        in_specs=[VMEM, VMEM, VMEM, SMEM, VMEM],
        out_specs=(VMEM, VMEM, VMEM),
        compiler_params=PARAMS,
        cost_estimate=cost(10_000_000, 1_000_000),
        name="weights",
    )(got, nominal, counts, step_lengths, own)
    position = jnp.stack([lax.axis_index("x"), lax.axis_index("y")]).astype(jnp.int32)
    term = pl.pallas_call(
        hessian_kernel,
        out_shape=jax.ShapeDtypeStruct((2, SIDE, SIDE, 64, LANES), BF16),
        in_specs=[SMEM] + [VMEM] * 8,
        out_specs=VMEM,
        scratch_shapes=[
            pltpu.VMEM((SIDE, DEPTH, LANES), BF16),
            pltpu.VMEM((SIDE, DEPTH, LANES), BF16),
        ],
        compiler_params=PARAMS,
        cost_estimate=cost(2_000_000_000, 5_000_000),
        name="hessian",
    )(position, weights, own, x1, x3, x2, y1, y3, y2)
    bins_sum = exchanged(bins_part, ("z", "core")).sum(axis=0)
    pair = exchanged(term.reshape(8, SIDE * 64, LANES), ("core", "y")).astype(F32)
    pair = pair.reshape(2, 16, 64, LANES).sum(axis=0).astype(BF16)
    tile = exchanged(pair, "z").astype(F32).sum(axis=0)
    square_sums = squares.sum(axis=1)[:4]
    change = bins_sum[1:4].sum(axis=1)
    line_change = (change + 0.5 * (square_sums[1:] - square_sums[0])) / bin_total
    gradient = (bins_sum[0] + start) / bin_total
    row_ids = (lax.axis_index("z") * 2 + lax.axis_index("core")) * 64
    row_ids = row_ids + jnp.arange(64, dtype=jnp.int32)
    col_ids = (lax.axis_index("y") * SIDE + lax.axis_index("x")) * LANES
    col_ids = col_ids + jnp.arange(LANES, dtype=jnp.int32)
    identity = (row_ids[:, None] == col_ids[None, :]).astype(F32)
    hessian = (tile + identity) / bin_total
    return line_change, gradient, hessian


def solution(mesh):
    split = Mesh(
        np.asarray(mesh.devices).reshape(16, 2, SIDE, SIDE), ("z", "core", "y", "x")
    )
    bins, nuis = ("z", "core"), ("y", "x")
    placed = (P(bins, None), P(bins, None, nuis), P(bins), P(nuis), P(nuis), P())
    return jax.shard_map(
        shards,
        mesh=split,
        in_specs=placed,
        out_specs=(P(), P(nuis), P(bins, nuis)),
        check_vma=False,
    )
```

```python
import jax
import jax.numpy as jnp
import numpy as np
from jax import lax
from jax.experimental import pallas as pl
from jax.experimental.pallas import tpu as pltpu
from jax.sharding import Mesh
from jax.sharding import PartitionSpec as P


F32 = jnp.float32
BF16 = jnp.bfloat16
SIDE = 4
PROC = 8
ROWS = 2048
BINS_DEV = 256
LANES = 128
CHUNKS = ROWS // LANES
BIN_TOTAL = 32 * BINS_DEV
DEPTH = ROWS + BINS_DEV
VMEM = pl.BlockSpec(memory_space=pltpu.VMEM)
SMEM = pl.BlockSpec(memory_space=pltpu.SMEM)
PARAMS = pltpu.CompilerParams(vmem_limit_bytes=48 * 1024 * 1024)


def cost(flops, moved):
    return pl.CostEstimate(flops=flops, bytes_accessed=moved, transcendentals=0)


def thirds(x):
    high = x.astype(BF16)
    rest = x - high.astype(F32)
    middle = rest.astype(BF16)
    low = (rest - middle.astype(F32)).astype(BF16)
    return [high, middle, low]


def rows_dot(a, b):
    return lax.dot_general(a, b, (((1,), (0,)), ((), ())), preferred_element_type=F32)


def packed(four):
    return jnp.concatenate(thirds(four) + [jnp.zeros((4, LANES), BF16)], 0)


def unpacked(rows):
    wide = rows.astype(F32)
    return wide[..., 0:4, :] + wide[..., 4:8, :] + wide[..., 8:12, :]


def project_kernel(v_ref, start_ref, dir_ref, steps_ref, out_ref, flat):
    start, direction = start_ref[...], dir_ref[...]
    parts = jnp.concatenate(thirds(start) + thirds(direction), 0)
    six = lax.dot_general(
        parts, v_ref[...], (((1,), (1,)), ((), ())), preferred_element_type=F32
    )
    along_start = six[0:1] + six[1:2] + six[2:3]
    along_dir = six[3:4] + six[4:5] + six[5:6]
    for c in range(CHUNKS):
        span = slice(c * LANES, (c + 1) * LANES)
        flat[c : c + 1, :] = along_start[:, span]
        flat[CHUNKS + c : CHUNKS + c + 1, :] = along_dir[:, span]
    flat[2 * CHUNKS : 2 * CHUNKS + 8, :] = jnp.zeros((8, LANES), F32)
    flat[2 * CHUNKS : 2 * CHUNKS + 1, :] = start * start
    for j in range(3):
        point = start + steps_ref[j] * direction
        flat[2 * CHUNKS + 1 + j : 2 * CHUNKS + 2 + j, :] = point * point
    whole = flat[...]
    for i in range(out_ref.shape[0]):
        out_ref[i] = whole


def lane_groups_sum(x, lane):
    for k in (1, 2, 4):
        up = pltpu.roll(x, k, 1)
        down = pltpu.roll(x, LANES - k, 1)
        x = x + jnp.where((lane & k) != 0, up, down)
    return x


def weights_kernel(got_ref, nominal_ref, counts_ref, steps_ref, v_ref, w_ref, bins_ref, sq_ref):
    total = jnp.sum(got_ref[...], axis=0)
    along_start = total[0:CHUNKS]
    along_dir = total[CHUNKS : 2 * CHUNKS]
    sq_ref[...] = total[2 * CHUNKS : 2 * CHUNKS + 8]
    nominal, counts = nominal_ref[...], counts_ref[...]
    lane = lax.broadcasted_iota(jnp.int32, (CHUNKS, LANES), 1)
    base = jnp.exp(nominal + along_start)
    base_total = lane_groups_sum(base, lane)
    base_log = jnp.log(base_total)
    part = [None] * 3
    for j in range(3):
        shifted = jnp.exp(nominal + (along_start + steps_ref[j] * along_dir))
        expected = lane_groups_sum(shifted, lane)
        change = (expected - base_total) - counts * (jnp.log(expected) - base_log)
        part[j] = jnp.sum(change, axis=0, keepdims=True) * (1.0 / PROC)
    residual = 1.0 - counts / base_total
    left = residual * base
    w_ref[0] = base
    w_ref[1] = left
    w_ref[2] = (counts / (base_total * base_total)) * base
    grad = jnp.zeros((3, LANES), F32)
    for c in range(CHUNKS):
        row = jnp.concatenate(thirds(left[c : c + 1]), 0)
        grad = grad + rows_dot(row, v_ref[c * LANES : (c + 1) * LANES, :])
    grad = jnp.sum(grad, axis=0, keepdims=True)
    bins_ref[...] = packed(jnp.concatenate([grad] + part, 0))


def hessian_kernel(pos_ref, w_ref, extra_ref, own, x1, x3, x2, y1, y3, y2, out_ref, rights, lefts):
    px, py = pos_ref[0], pos_ref[1]
    mine = lax.broadcasted_iota(jnp.int32, (16, LANES), 1) // PROC
    mine = mine == lax.broadcasted_iota(jnp.int32, (16, LANES), 0)
    columns = w_ref[1].T
    for c in range(CHUNKS):
        span = slice(c * LANES, (c + 1) * LANES)
        jac_span = slice(ROWS + c * 16, ROWS + (c + 1) * 16)
        both = []
        for k in (0, 2):
            spread = jnp.where(mine, w_ref[k, c : c + 1, :], 0.0)
            both.append(jnp.concatenate(thirds(spread), 0))
        scale = columns[:, c : c + 1]
        for step, ref in enumerate((own, x1, x2, x3)):
            at = lax.rem(px + step, SIDE)
            rows = ref[span, :]
            rights[at, span, :] = rows
            jac = rows_dot(both[0], rows)
            rights[at, jac_span, :] = (jac[0:16] + jac[16:32] + jac[32:48]).astype(BF16)
        for step, ref in enumerate((own, y1, y2, y3)):
            at = lax.rem(py + step, SIDE)
            rows = ref[span, :]
            lefts[at, span, :] = (scale * rows.astype(F32)).astype(BF16)
            jac = rows_dot(both[1], rows)
            lefts[at, jac_span, :] = (jac[0:16] + jac[16:32] + jac[32:48]).astype(BF16)
    right = jnp.concatenate([rights[k] for k in range(SIDE)], 1)
    for j in range(SIDE):
        term = lax.dot_general(
            right, lefts[j], (((0,), (0,)), ((), ())), preferred_element_type=F32
        ).astype(BF16)
        for half in range(2):
            for i in range(SIDE):
                at = i * LANES + half * 64
                out_ref[half * SIDE + j, i * 64 : (i + 1) * 64, :] = term[at : at + 64]
            out_ref[half * SIDE + j, SIDE * 64 :, :] = extra_ref[...]


def fold_kernel(pos_ref, got_ref, out_ref):
    py = pos_ref[1]
    extra = unpacked(got_ref[py, SIDE * 64 :, :]) + unpacked(got_ref[SIDE + py, SIDE * 64 :, :])
    extra = packed(extra)
    for k in range(SIDE):
        for i in range(SIDE):
            span = slice(i * 64, (i + 1) * 64)
            both = got_ref[k, span, :].astype(F32) + got_ref[SIDE + k, span, :].astype(F32)
            out_ref[k * SIDE + i, 0:64, :] = both.astype(BF16)
            out_ref[k * SIDE + i, 64:, :] = extra


def finish_kernel(pos_ref, got_ref, sq_ref, start_ref, line_ref, grad_ref, hess_ref):
    scale = 1.0 / BIN_TOTAL
    tile = jnp.sum(got_ref[:, 0:64, :].astype(F32), axis=0)
    extra = jnp.sum(unpacked(got_ref[:, 64:, :]), axis=0)
    row = lax.broadcasted_iota(jnp.int32, (64, LANES), 0) + pos_ref[2] * 64
    col = lax.broadcasted_iota(jnp.int32, (64, LANES), 1) + pos_ref[3] * LANES
    hess_ref[...] = (tile + (row == col).astype(F32)) * scale
    grad_ref[...] = (extra[0:1] + start_ref[...]) * scale
    for j in range(3):
        squares = sq_ref[1 + j : 2 + j, :] - sq_ref[0:1, :]
        line_ref[j] = jnp.sum(extra[1 + j : 2 + j, :] + 0.5 * squares) * scale


def arrays_of(*shapes):
    return tuple(jax.ShapeDtypeStruct(s, d) for s, d in shapes)


def from_ahead(array, axis, step):
    return lax.ppermute(array, axis, [((i + step) % SIDE, i) for i in range(SIDE)])


def exchanged(array, axes):
    return lax.all_to_all(array, axes, 0, 0, tiled=True)


def body(log_nominal, variations, observed, start, direction, step_lengths):
    own = variations.reshape(ROWS, LANES)
    y3, x3, y1, x1, y2, x2 = (
        from_ahead(own, axis, k) for k in (3, 1, 2) for axis in ("y", "x")
    )
    sent = pl.pallas_call(
        project_kernel,
        out_shape=jax.ShapeDtypeStruct((16, 40, LANES), F32),
        in_specs=[VMEM, VMEM, VMEM, SMEM],
        out_specs=VMEM,
        scratch_shapes=[pltpu.VMEM((40, LANES), F32)],
        compiler_params=PARAMS,
        cost_estimate=cost(10_000_000, 1_000_000),
        name="project",
    )(own, start[None, :], direction[None, :], step_lengths)
    got = exchanged(sent, ("y", "x"))
    nominal = log_nominal.reshape(CHUNKS, LANES)
    counts = jnp.repeat(observed.astype(F32), PROC).reshape(CHUNKS, LANES)
    weights, extra, squares = pl.pallas_call(
        weights_kernel,
        out_shape=arrays_of(
            ((3, CHUNKS, LANES), F32), ((16, LANES), BF16), ((8, LANES), F32)
        ),
        in_specs=[VMEM, VMEM, VMEM, SMEM, VMEM],
        out_specs=(VMEM, VMEM, VMEM),
        compiler_params=PARAMS,
        cost_estimate=cost(10_000_000, 1_000_000),
        name="weights",
    )(got, nominal, counts, step_lengths, own)
    px, py = lax.axis_index("x"), lax.axis_index("y")
    block = lax.axis_index("z") * 2 + lax.axis_index("core")
    position = jnp.stack([px, py, block, py * SIDE + px]).astype(jnp.int32)
    term = pl.pallas_call(
        hessian_kernel,
        out_shape=jax.ShapeDtypeStruct((8, SIDE * 64 + 16, LANES), BF16),
        in_specs=[SMEM] + [VMEM] * 9,
        out_specs=VMEM,
        scratch_shapes=[
            pltpu.VMEM((SIDE, DEPTH, LANES), BF16),
            pltpu.VMEM((SIDE, DEPTH, LANES), BF16),
        ],
        compiler_params=PARAMS,
        cost_estimate=cost(2_000_000_000, 5_000_000),
        name="hessian",
    )(position, weights, extra, own, x1, x3, x2, y1, y3, y2)
    pair = pl.pallas_call(
        fold_kernel,
        out_shape=jax.ShapeDtypeStruct((16, 80, LANES), BF16),
        in_specs=[SMEM, VMEM],
        out_specs=VMEM,
        compiler_params=PARAMS,
        cost_estimate=cost(1_000_000, 1_000_000),
        name="fold",
    )(position, exchanged(term, ("core", "y")))
    line_change, gradient, hessian = pl.pallas_call(
        finish_kernel,
        out_shape=arrays_of(((3,), F32), ((1, LANES), F32), ((64, LANES), F32)),
        in_specs=[SMEM, VMEM, VMEM, VMEM],
        out_specs=(SMEM, VMEM, VMEM),
        compiler_params=PARAMS,
        cost_estimate=cost(1_000_000, 1_000_000),
        name="finish",
    )(position, exchanged(pair, "z"), squares, start[None, :])
    return line_change, gradient[0], hessian


def solution(mesh):
    split = Mesh(
        np.asarray(mesh.devices).reshape(16, 2, SIDE, SIDE), ("z", "core", "y", "x")
    )
    bins, nuis = ("z", "core"), ("y", "x")
    placed = (P(bins, None), P(bins, None, nuis), P(bins), P(nuis), P(nuis), P())
    return jax.shard_map(
        body,
        mesh=split,
        in_specs=placed,
        out_specs=(P(), P(nuis), P(bins, nuis)),
        check_vma=False,
    )
```

```python
import jax
import jax.numpy as jnp
import numpy as np
from jax import lax
from jax.experimental import pallas as pl
from jax.experimental.pallas import tpu as pltpu
from jax.sharding import Mesh
from jax.sharding import PartitionSpec as P


F32 = jnp.float32
BF16 = jnp.bfloat16
SIDE = 4
PROC = 8
ROWS = 2048
BINS_DEV = 256
LANES = 128
CHUNKS = ROWS // LANES
PIECES = SIDE * SIDE
BIN_TOTAL = 32 * BINS_DEV
DEPTH = ROWS + BINS_DEV
VMEM = pl.BlockSpec(memory_space=pltpu.VMEM)
SMEM = pl.BlockSpec(memory_space=pltpu.SMEM)
PARAMS = pltpu.CompilerParams(vmem_limit_bytes=48 * 1024 * 1024)


def cost(flops, moved):
    return pl.CostEstimate(flops=flops, bytes_accessed=moved, transcendentals=0)


def thirds(x):
    high = x.astype(BF16)
    rest = x - high.astype(F32)
    middle = rest.astype(BF16)
    low = (rest - middle.astype(F32)).astype(BF16)
    return [high, middle, low]


def rows_dot(a, b):
    return lax.dot_general(a, b, (((1,), (0,)), ((), ())), preferred_element_type=F32)


def packed(four):
    return jnp.concatenate(thirds(four) + [jnp.zeros((4, LANES), BF16)], 0)


def unpacked(rows):
    wide = rows.astype(F32)
    return wide[..., 0:4, :] + wide[..., 4:8, :] + wide[..., 8:12, :]


def project_kernel(v_ref, start_ref, dir_ref, steps_ref, out_ref, flat):
    start, direction = start_ref[...], dir_ref[...]
    parts = jnp.concatenate(thirds(start) + thirds(direction), 0)
    six = lax.dot_general(
        parts, v_ref[...], (((1,), (1,)), ((), ())), preferred_element_type=F32
    )
    along_start = six[0:1] + six[1:2] + six[2:3]
    along_dir = six[3:4] + six[4:5] + six[5:6]
    for c in range(CHUNKS):
        span = slice(c * LANES, (c + 1) * LANES)
        flat[c : c + 1, :] = along_start[:, span]
        flat[CHUNKS + c : CHUNKS + c + 1, :] = along_dir[:, span]
    flat[2 * CHUNKS : 2 * CHUNKS + 8, :] = jnp.zeros((8, LANES), F32)
    flat[2 * CHUNKS : 2 * CHUNKS + 1, :] = start * start
    for j in range(3):
        point = start + steps_ref[j] * direction
        flat[2 * CHUNKS + 1 + j : 2 * CHUNKS + 2 + j, :] = point * point
    whole = flat[...]
    for i in range(out_ref.shape[0]):
        out_ref[i] = whole


def lane_groups_sum(x, lane):
    for k in (1, 2, 4):
        up = pltpu.roll(x, k, 1)
        down = pltpu.roll(x, LANES - k, 1)
        x = x + jnp.where((lane & k) != 0, up, down)
    return x


def weights_kernel(got_ref, nominal_ref, counts_ref, steps_ref, v_ref, w_ref, bins_ref, sq_ref):
    total = jnp.sum(got_ref[...], axis=0)
    along_start = total[0:CHUNKS]
    along_dir = total[CHUNKS : 2 * CHUNKS]
    sq_ref[...] = total[2 * CHUNKS : 2 * CHUNKS + 8]
    nominal, counts = nominal_ref[...], counts_ref[...]
    lane = lax.broadcasted_iota(jnp.int32, (CHUNKS, LANES), 1)
    base = jnp.exp(nominal + along_start)
    base_total = lane_groups_sum(base, lane)
    base_log = jnp.log(base_total)
    part = [None] * 3
    for j in range(3):
        shifted = jnp.exp(nominal + (along_start + steps_ref[j] * along_dir))
        expected = lane_groups_sum(shifted, lane)
        change = (expected - base_total) - counts * (jnp.log(expected) - base_log)
        part[j] = jnp.sum(change, axis=0, keepdims=True) * (1.0 / PROC)
    residual = 1.0 - counts / base_total
    left = residual * base
    w_ref[0] = base
    w_ref[1] = left
    w_ref[2] = (counts / (base_total * base_total)) * base
    grad = jnp.zeros((3, LANES), F32)
    for c in range(CHUNKS):
        row = jnp.concatenate(thirds(left[c : c + 1]), 0)
        grad = grad + rows_dot(row, v_ref[c * LANES : (c + 1) * LANES, :])
    grad = jnp.sum(grad, axis=0, keepdims=True)
    bins_ref[...] = packed(jnp.concatenate([grad] + part, 0))


def hessian_kernel(
    pos_ref, w_ref, extra_ref, own, x1, y1, x3, y3, x2, y2, kept_ref, sent_ref, rights, lefts
):
    px, py, core = pos_ref[0], pos_ref[1], pos_ref[4]
    mine = lax.broadcasted_iota(jnp.int32, (16, LANES), 1) // PROC
    mine = mine == lax.broadcasted_iota(jnp.int32, (16, LANES), 0)
    columns = w_ref[1].T
    for c in range(CHUNKS):
        span = slice(c * LANES, (c + 1) * LANES)
        jac_span = slice(ROWS + c * 16, ROWS + (c + 1) * 16)
        both = []
        for k in (0, 2):
            spread = jnp.where(mine, w_ref[k, c : c + 1, :], 0.0)
            both.append(jnp.concatenate(thirds(spread), 0))
        scale = columns[:, c : c + 1]
        for step, ref in enumerate((own, x1, x2, x3)):
            at = lax.rem(px + step, SIDE)
            rows = ref[span, :]
            rights[at, span, :] = rows
            jac = rows_dot(both[0], rows)
            rights[at, jac_span, :] = (jac[0:16] + jac[16:32] + jac[32:48]).astype(BF16)
        for step, ref in enumerate((own, y1, y2, y3)):
            at = lax.rem(py + step, SIDE)
            rows = ref[span, :]
            lefts[at, span, :] = (scale * rows.astype(F32)).astype(BF16)
            jac = rows_dot(both[1], rows)
            lefts[at, jac_span, :] = (jac[0:16] + jac[16:32] + jac[32:48]).astype(BF16)
    right = jnp.concatenate([rights[k] for k in range(SIDE)], 1)
    for j in range(SIDE):
        term = lax.dot_general(
            right, lefts[j], (((0,), (0,)), ((), ())), preferred_element_type=F32
        )
        for i in range(SIDE):
            first = term[i * LANES : i * LANES + 64]
            second = term[i * LANES + 64 : (i + 1) * LANES]
            at = (i * SIDE + j) * 64
            kept_ref[at : at + 64, :] = jnp.where(core == 0, first, second)
            sent_ref[at : at + 64, :] = jnp.where(core == 0, second, first).astype(BF16)
    sent_ref[PIECES * 64 :, :] = extra_ref[...]


def pair_kernel(kept_ref, extra_ref, got_ref, out_ref):
    extra = packed(unpacked(extra_ref[...]) + unpacked(got_ref[PIECES * 64 :, :]))
    for k in range(PIECES):
        span = slice(k * 64, (k + 1) * 64)
        both = kept_ref[span, :] + got_ref[span, :].astype(F32)
        out_ref[k, 0:64, :] = both.astype(BF16)
        out_ref[k, 64:, :] = extra


def plane_kernel(pos_ref, got_ref, out_ref):
    py = pos_ref[1]
    extra = unpacked(got_ref[py, 64:, :])
    for k in range(1, SIDE):
        extra = extra + unpacked(got_ref[k * SIDE + py, 64:, :])
    extra = packed(extra)
    for j in range(SIDE):
        tile = got_ref[j, 0:64, :].astype(F32)
        for k in range(1, SIDE):
            tile = tile + got_ref[k * SIDE + j, 0:64, :].astype(F32)
        out_ref[j, 0:64, :] = tile.astype(BF16)
        out_ref[j, 64:, :] = extra


def finish_kernel(pos_ref, got_ref, sq_ref, start_ref, line_ref, grad_ref, hess_ref):
    scale = 1.0 / BIN_TOTAL
    tile = jnp.sum(got_ref[:, 0:64, :].astype(F32), axis=0)
    extra = jnp.sum(unpacked(got_ref[:, 64:, :]), axis=0)
    row = lax.broadcasted_iota(jnp.int32, (64, LANES), 0) + pos_ref[2] * 64
    col = lax.broadcasted_iota(jnp.int32, (64, LANES), 1) + pos_ref[3] * LANES
    hess_ref[...] = (tile + (row == col).astype(F32)) * scale
    grad_ref[...] = (extra[0:1] + start_ref[...]) * scale
    for j in range(3):
        squares = sq_ref[1 + j : 2 + j, :] - sq_ref[0:1, :]
        line_ref[j] = jnp.sum(extra[1 + j : 2 + j, :] + 0.5 * squares) * scale


def arrays_of(*shapes):
    return tuple(jax.ShapeDtypeStruct(s, d) for s, d in shapes)


def from_ahead(array, axis, step):
    return lax.ppermute(array, axis, [((i + step) % SIDE, i) for i in range(SIDE)])


def exchanged(array, axes):
    return lax.all_to_all(array, axes, 0, 0, tiled=True)


def body(log_nominal, variations, observed, start, direction, step_lengths):
    own = variations.reshape(ROWS, LANES)
    y3, x3, y1, x1, y2, x2 = (
        from_ahead(own, axis, k) for k in (3, 1, 2) for axis in ("y", "x")
    )
    sent = pl.pallas_call(
        project_kernel,
        out_shape=jax.ShapeDtypeStruct((16, 40, LANES), F32),
        in_specs=[VMEM, VMEM, VMEM, SMEM],
        out_specs=VMEM,
        scratch_shapes=[pltpu.VMEM((40, LANES), F32)],
        compiler_params=PARAMS,
        cost_estimate=cost(10_000_000, 1_000_000),
        name="project",
    )(own, start[None, :], direction[None, :], step_lengths)
    got = exchanged(sent, ("y", "x"))
    nominal = log_nominal.reshape(CHUNKS, LANES)
    counts = jnp.repeat(observed.astype(F32), PROC).reshape(CHUNKS, LANES)
    weights, extra, squares = pl.pallas_call(
        weights_kernel,
        out_shape=arrays_of(
            ((3, CHUNKS, LANES), F32), ((16, LANES), BF16), ((8, LANES), F32)
        ),
        in_specs=[VMEM, VMEM, VMEM, SMEM, VMEM],
        out_specs=(VMEM, VMEM, VMEM),
        compiler_params=PARAMS,
        cost_estimate=cost(10_000_000, 1_000_000),
        name="weights",
    )(got, nominal, counts, step_lengths, own)
    px, py = lax.axis_index("x"), lax.axis_index("y")
    core = lax.axis_index("core")
    block = lax.axis_index(("zh", "zl", "core"))
    position = jnp.stack([px, py, block, py * SIDE + px, core]).astype(jnp.int32)
    kept, other = pl.pallas_call(
        hessian_kernel,
        out_shape=arrays_of(
            ((PIECES * 64, LANES), F32), ((PIECES * 64 + 16, LANES), BF16)
        ),
        in_specs=[SMEM] + [VMEM] * 9,
        out_specs=(VMEM, VMEM),
        scratch_shapes=[
            pltpu.VMEM((SIDE, DEPTH, LANES), BF16),
            pltpu.VMEM((SIDE, DEPTH, LANES), BF16),
        ],
        compiler_params=PARAMS,
        cost_estimate=cost(2_000_000_000, 5_000_000),
        name="hessian",
    )(position, weights, extra, own, x1, y1, x3, y3, x2, y2)
    swapped = lax.ppermute(other, "core", [(0, 1), (1, 0)])
    pair = pl.pallas_call(
        pair_kernel,
        out_shape=jax.ShapeDtypeStruct((PIECES, 80, LANES), BF16),
        in_specs=[VMEM] * 3,
        out_specs=VMEM,
        compiler_params=PARAMS,
        cost_estimate=cost(1_000_000, 1_000_000),
        name="pair",
    )(kept, extra, swapped)
    near = pl.pallas_call(
        plane_kernel,
        out_shape=jax.ShapeDtypeStruct((SIDE, 80, LANES), BF16),
        in_specs=[SMEM, VMEM],
        out_specs=VMEM,
        compiler_params=PARAMS,
        cost_estimate=cost(1_000_000, 1_000_000),
        name="plane",
    )(position, exchanged(pair, ("zl", "y")))
    line_change, gradient, hessian = pl.pallas_call(
        finish_kernel,
        out_shape=arrays_of(((3,), F32), ((1, LANES), F32), ((64, LANES), F32)),
        in_specs=[SMEM, VMEM, VMEM, VMEM],
        out_specs=(SMEM, VMEM, VMEM),
        compiler_params=PARAMS,
        cost_estimate=cost(1_000_000, 1_000_000),
        name="finish",
    )(position, exchanged(near, "zh"), squares, start[None, :])
    return line_change, gradient[0], hessian


def solution(mesh):
    split = Mesh(
        np.asarray(mesh.devices).reshape(SIDE, SIDE, 2, SIDE, SIDE),
        ("zh", "zl", "core", "y", "x"),
    )
    bins, nuis = ("zh", "zl", "core"), ("y", "x")
    placed = (P(bins, None), P(bins, None, nuis), P(bins), P(nuis), P(nuis), P())
    return jax.shard_map(
        body,
        mesh=split,
        in_specs=placed,
        out_specs=(P(), P(nuis), P(bins, nuis)),
        check_vma=False,
    )
```

```python
import jax
import jax.numpy as jnp
import numpy as np
from jax import lax
from jax.experimental import pallas as pl
from jax.experimental.pallas import tpu as pltpu
from jax.sharding import Mesh
from jax.sharding import PartitionSpec as P


F32 = jnp.float32
BF16 = jnp.bfloat16
SIDE = 4
PROC = 8
ROWS = 2048
BINS_DEV = 256
LANES = 128
CHUNKS = ROWS // LANES
PIECES = SIDE * SIDE
BIN_TOTAL = 32 * BINS_DEV
DEPTH = ROWS + BINS_DEV
VMEM = pl.BlockSpec(memory_space=pltpu.VMEM)
SMEM = pl.BlockSpec(memory_space=pltpu.SMEM)
PARAMS = pltpu.CompilerParams(vmem_limit_bytes=48 * 1024 * 1024)


def cost(flops, moved):
    return pl.CostEstimate(flops=flops, bytes_accessed=moved, transcendentals=0)


def thirds(x):
    high = x.astype(BF16)
    rest = x - high.astype(F32)
    middle = rest.astype(BF16)
    low = (rest - middle.astype(F32)).astype(BF16)
    return [high, middle, low]


def rows_dot(a, b):
    return lax.dot_general(a, b, (((1,), (0,)), ((), ())), preferred_element_type=F32)


def packed(four):
    return jnp.concatenate(thirds(four) + [jnp.zeros((4, LANES), BF16)], 0)


def unpacked(rows):
    wide = rows.astype(F32)
    return wide[..., 0:4, :] + wide[..., 4:8, :] + wide[..., 8:12, :]


def project_kernel(v_ref, start_ref, dir_ref, steps_ref, out_ref, flat):
    start, direction = start_ref[...], dir_ref[...]
    parts = jnp.concatenate(thirds(start) + thirds(direction), 0)
    six = lax.dot_general(
        parts, v_ref[...], (((1,), (1,)), ((), ())), preferred_element_type=F32
    )
    along_start = six[0:1] + six[1:2] + six[2:3]
    along_dir = six[3:4] + six[4:5] + six[5:6]
    for c in range(CHUNKS):
        span = slice(c * LANES, (c + 1) * LANES)
        flat[c : c + 1, :] = along_start[:, span]
        flat[CHUNKS + c : CHUNKS + c + 1, :] = along_dir[:, span]
    flat[2 * CHUNKS : 2 * CHUNKS + 8, :] = jnp.zeros((8, LANES), F32)
    flat[2 * CHUNKS : 2 * CHUNKS + 1, :] = start * start
    for j in range(3):
        point = start + steps_ref[j] * direction
        flat[2 * CHUNKS + 1 + j : 2 * CHUNKS + 2 + j, :] = point * point
    whole = flat[...]
    for i in range(out_ref.shape[0]):
        out_ref[i] = whole


def lane_groups_sum(x, lane):
    for k in (1, 2, 4):
        up = pltpu.roll(x, k, 1)
        down = pltpu.roll(x, LANES - k, 1)
        x = x + jnp.where((lane & k) != 0, up, down)
    return x


def by_row(nominal, counts, lane):
    place = lax.broadcasted_iota(jnp.int32, (CHUNKS, BINS_DEV), 1)
    line = lax.broadcasted_iota(jnp.int32, (CHUNKS, BINS_DEV), 0)
    mine = place // CHUNKS == line
    each = [nominal[p : p + 1] for p in range(PROC)] + [counts]
    spread = jnp.concatenate([jnp.where(mine, row, 0.0) for row in each], 0)
    source = lax.broadcasted_iota(jnp.int32, (BINS_DEV, LANES), 0) % CHUNKS
    target = lax.broadcasted_iota(jnp.int32, (BINS_DEV, LANES), 1) // PROC
    pick = (source == target).astype(F32).astype(BF16)
    high, middle, low = (rows_dot(part, pick) for part in thirds(spread))
    moved = high + middle + low
    out = jnp.zeros((CHUNKS, LANES), F32)
    for p in range(PROC):
        out = jnp.where(lane % PROC == p, moved[p * CHUNKS : (p + 1) * CHUNKS], out)
    return out, moved[PROC * CHUNKS :]


def weights_kernel(got_ref, nominal_ref, counts_ref, steps_ref, v_ref, w_ref, bins_ref, sq_ref):
    total = jnp.sum(got_ref[...], axis=0)
    along_start = total[0:CHUNKS]
    along_dir = total[CHUNKS : 2 * CHUNKS]
    sq_ref[...] = total[2 * CHUNKS : 2 * CHUNKS + 8]
    lane = lax.broadcasted_iota(jnp.int32, (CHUNKS, LANES), 1)
    nominal, counts = by_row(nominal_ref[...], counts_ref[...].astype(F32), lane)
    base = jnp.exp(nominal + along_start)
    base_total = lane_groups_sum(base, lane)
    base_log = jnp.log(base_total)
    part = [None] * 3
    for j in range(3):
        shifted = jnp.exp(nominal + (along_start + steps_ref[j] * along_dir))
        expected = lane_groups_sum(shifted, lane)
        change = (expected - base_total) - counts * (jnp.log(expected) - base_log)
        part[j] = jnp.sum(change, axis=0, keepdims=True) * (1.0 / PROC)
    residual = 1.0 - counts / base_total
    left = residual * base
    w_ref[0] = base
    w_ref[1] = left
    w_ref[2] = (counts / (base_total * base_total)) * base
    grad = jnp.zeros((3, LANES), F32)
    for c in range(CHUNKS):
        row = jnp.concatenate(thirds(left[c : c + 1]), 0)
        grad = grad + rows_dot(row, v_ref[c * LANES : (c + 1) * LANES, :])
    grad = jnp.sum(grad, axis=0, keepdims=True)
    bins_ref[...] = packed(jnp.concatenate([grad] + part, 0))


def hessian_kernel(
    pos_ref, w_ref, extra_ref, own, x1, y1, x3, y3, x2, y2, kept_ref, sent_ref,
    right_t, left, jac_rows,
):
    px, py, core = pos_ref[0], pos_ref[1], pos_ref[4]
    mine = lax.broadcasted_iota(jnp.int32, (16, LANES), 1) // PROC
    mine = mine == lax.broadcasted_iota(jnp.int32, (16, LANES), 0)

    def spot(at):
        return pl.ds(pl.multiple_of(at * LANES, LANES), LANES)

    def chunk(c, carry):
        span = spot(c)
        jac_span = pl.ds(pl.multiple_of(ROWS + c * 16, 16), 16)

        def spread(k):
            return jnp.concatenate(thirds(jnp.where(mine, w_ref[k, pl.ds(c, 1), :], 0.0)), 0)

        def summed(jac):
            return (jac[0:16] + jac[16:32] + jac[32:48]).astype(BF16)

        across = [ref[span, :] for ref in (own, x1, x2, x3)]
        jac = summed(rows_dot(spread(0), jnp.concatenate(across, 1)))
        for step, rows in enumerate(across):
            at = lax.rem(px + step, SIDE)
            right_t[spot(at), span] = rows.T
            jac_at = pl.ds(pl.multiple_of(at * BINS_DEV + c * 16, 16), 16)
            jac_rows[jac_at, :] = jac[:, step * LANES : (step + 1) * LANES]
        down = [ref[span, :] for ref in (own, y1, y2, y3)]
        jac = summed(rows_dot(spread(2), jnp.concatenate(down, 1)))
        scale = jnp.broadcast_to(w_ref[1, pl.ds(c, 1), :], (LANES, LANES)).T
        for step, rows in enumerate(down):
            at = spot(lax.rem(py + step, SIDE))
            left[span, at] = (scale * rows.astype(F32)).astype(BF16)
            left[jac_span, at] = jac[:, step * LANES : (step + 1) * LANES]
        return carry

    lax.fori_loop(0, CHUNKS, chunk, 0, unroll=2)
    for i in range(SIDE):
        rows = jac_rows[i * BINS_DEV : (i + 1) * BINS_DEV, :]
        right_t[i * LANES : (i + 1) * LANES, ROWS:] = rows.T
    for n in range(2):
        term = rows_dot(right_t[...], left[:, n * 2 * LANES : (n + 1) * 2 * LANES])
        for i in range(SIDE):
            for half in range(2):
                part = term[:, half * LANES : (half + 1) * LANES]
                first = part[i * LANES : i * LANES + 64]
                second = part[i * LANES + 64 : (i + 1) * LANES]
                at = (i * SIDE + 2 * n + half) * 64
                kept_ref[at : at + 64, :] = jnp.where(core == 0, first, second)
                sent_ref[at : at + 64, :] = jnp.where(core == 0, second, first).astype(BF16)
    sent_ref[PIECES * 64 :, :] = extra_ref[...]


def pair_kernel(kept_ref, extra_ref, got_ref, out_ref):
    extra = packed(unpacked(extra_ref[...]) + unpacked(got_ref[PIECES * 64 :, :]))
    for k in range(PIECES):
        span = slice(k * 64, (k + 1) * 64)
        both = kept_ref[span, :] + got_ref[span, :].astype(F32)
        out_ref[k, 0:64, :] = both.astype(BF16)
        out_ref[k, 64:, :] = extra


def plane_kernel(pos_ref, got_ref, out_ref):
    py = pos_ref[1]
    extra = unpacked(got_ref[py, 64:, :])
    for k in range(1, SIDE):
        extra = extra + unpacked(got_ref[k * SIDE + py, 64:, :])
    extra = packed(extra)
    for j in range(SIDE):
        tile = got_ref[j, 0:64, :].astype(F32)
        for k in range(1, SIDE):
            tile = tile + got_ref[k * SIDE + j, 0:64, :].astype(F32)
        out_ref[j, 0:64, :] = tile.astype(BF16)
        out_ref[j, 64:, :] = extra


def finish_kernel(pos_ref, got_ref, sq_ref, start_ref, line_ref, grad_ref, hess_ref):
    scale = 1.0 / BIN_TOTAL
    tile = jnp.sum(got_ref[:, 0:64, :].astype(F32), axis=0)
    extra = jnp.sum(unpacked(got_ref[:, 64:, :]), axis=0)
    row = lax.broadcasted_iota(jnp.int32, (64, LANES), 0) + pos_ref[2] * 64
    col = lax.broadcasted_iota(jnp.int32, (64, LANES), 1) + pos_ref[3] * LANES
    hess_ref[...] = (tile + (row == col).astype(F32)) * scale
    grad_ref[...] = (extra[0:1] + start_ref[...]) * scale
    for j in range(3):
        squares = sq_ref[1 + j : 2 + j, :] - sq_ref[0:1, :]
        line_ref[j] = jnp.sum(extra[1 + j : 2 + j, :] + 0.5 * squares) * scale


def arrays_of(*shapes):
    return tuple(jax.ShapeDtypeStruct(s, d) for s, d in shapes)


def from_ahead(array, axis, step):
    return lax.ppermute(array, axis, [((i + step) % SIDE, i) for i in range(SIDE)])


def exchanged(array, axes):
    return lax.all_to_all(array, axes, 0, 0, tiled=True)


def body(log_nominal, variations, observed, start, direction, step_lengths):
    own = variations.reshape(ROWS, LANES)
    y3, x3, y1, x1, y2, x2 = (
        from_ahead(own, axis, k) for k in (3, 1, 2) for axis in ("y", "x")
    )
    sent = pl.pallas_call(
        project_kernel,
        out_shape=jax.ShapeDtypeStruct((16, 40, LANES), F32),
        in_specs=[VMEM, VMEM, VMEM, SMEM],
        out_specs=VMEM,
        scratch_shapes=[pltpu.VMEM((40, LANES), F32)],
        compiler_params=PARAMS,
        cost_estimate=cost(10_000_000, 1_000_000),
        name="project",
    )(own, start[None, :], direction[None, :], step_lengths)
    got = exchanged(sent, ("y", "x"))
    weights, extra, squares = pl.pallas_call(
        weights_kernel,
        out_shape=arrays_of(
            ((3, CHUNKS, LANES), F32), ((16, LANES), BF16), ((8, LANES), F32)
        ),
        in_specs=[VMEM, VMEM, VMEM, SMEM, VMEM],
        out_specs=(VMEM, VMEM, VMEM),
        compiler_params=PARAMS,
        cost_estimate=cost(10_000_000, 1_000_000),
        name="weights",
    )(got, log_nominal.T, observed[None, :], step_lengths, own)
    px, py = lax.axis_index("x"), lax.axis_index("y")
    core = lax.axis_index("core")
    block = lax.axis_index(("zh", "zl", "core"))
    position = jnp.stack([px, py, block, py * SIDE + px, core]).astype(jnp.int32)
    kept, other = pl.pallas_call(
        hessian_kernel,
        out_shape=arrays_of(
            ((PIECES * 64, LANES), F32), ((PIECES * 64 + 16, LANES), BF16)
        ),
        in_specs=[SMEM] + [VMEM] * 9,
        out_specs=(VMEM, VMEM),
        scratch_shapes=[
            pltpu.VMEM((SIDE * LANES, DEPTH), BF16),
            pltpu.VMEM((DEPTH, SIDE * LANES), BF16),
            pltpu.VMEM((SIDE * BINS_DEV, LANES), BF16),
        ],
        compiler_params=PARAMS,
        cost_estimate=cost(2_000_000_000, 5_000_000),
        name="hessian",
    )(position, weights, extra, own, x1, y1, x3, y3, x2, y2)
    swapped = lax.ppermute(other, "core", [(0, 1), (1, 0)])
    pair = pl.pallas_call(
        pair_kernel,
        out_shape=jax.ShapeDtypeStruct((PIECES, 80, LANES), BF16),
        in_specs=[VMEM] * 3,
        out_specs=VMEM,
        compiler_params=PARAMS,
        cost_estimate=cost(1_000_000, 1_000_000),
        name="pair",
    )(kept, extra, swapped)
    near = pl.pallas_call(
        plane_kernel,
        out_shape=jax.ShapeDtypeStruct((SIDE, 80, LANES), BF16),
        in_specs=[SMEM, VMEM],
        out_specs=VMEM,
        compiler_params=PARAMS,
        cost_estimate=cost(1_000_000, 1_000_000),
        name="plane",
    )(position, exchanged(pair, ("zl", "y")))
    line_change, gradient, hessian = pl.pallas_call(
        finish_kernel,
        out_shape=arrays_of(((3,), F32), ((1, LANES), F32), ((64, LANES), F32)),
        in_specs=[SMEM, VMEM, VMEM, VMEM],
        out_specs=(SMEM, VMEM, VMEM),
        compiler_params=PARAMS,
        cost_estimate=cost(1_000_000, 1_000_000),
        name="finish",
    )(position, exchanged(near, "zh"), squares, start[None, :])
    return line_change, gradient[0], hessian


def solution(mesh):
    split = Mesh(
        np.asarray(mesh.devices).reshape(SIDE, SIDE, 2, SIDE, SIDE),
        ("zh", "zl", "core", "y", "x"),
    )
    bins, nuis = ("zh", "zl", "core"), ("y", "x")
    placed = (P(bins, None), P(bins, None, nuis), P(bins), P(nuis), P(nuis), P())
    return jax.shard_map(
        body,
        mesh=split,
        in_specs=placed,
        out_specs=(P(), P(nuis), P(bins, nuis)),
        check_vma=False,
    )
```

```python
import jax
import jax.numpy as jnp
import numpy as np
from jax import lax
from jax.experimental import pallas as pl
from jax.experimental.pallas import tpu as pltpu
from jax.sharding import Mesh
from jax.sharding import PartitionSpec as P


F32 = jnp.float32
BF16 = jnp.bfloat16
SIDE = 4
PROC = 8
ROWS = 2048
BINS_DEV = 256
LANES = 128
CHUNKS = ROWS // LANES
PIECES = SIDE * SIDE
BIN_TOTAL = 32 * BINS_DEV
DEPTH = ROWS + BINS_DEV
VMEM = pl.BlockSpec(memory_space=pltpu.VMEM)
SMEM = pl.BlockSpec(memory_space=pltpu.SMEM)
PARAMS = pltpu.CompilerParams(vmem_limit_bytes=16 * 1024 * 1024)


def cost(flops, moved):
    return pl.CostEstimate(flops=flops, bytes_accessed=moved, transcendentals=0)


def thirds(x):
    high = x.astype(BF16)
    rest = x - high.astype(F32)
    middle = rest.astype(BF16)
    low = (rest - middle.astype(F32)).astype(BF16)
    return [high, middle, low]


def rows_dot(a, b):
    return lax.dot_general(a, b, (((1,), (0,)), ((), ())), preferred_element_type=F32)


def packed(four):
    return jnp.concatenate(thirds(four) + [jnp.zeros((4, LANES), BF16)], 0)


def unpacked(rows):
    wide = rows.astype(F32)
    return wide[..., 0:4, :] + wide[..., 4:8, :] + wide[..., 8:12, :]


def pack_kernel(v_ref, start_ref, dir_ref, out_ref):
    out_ref[0:ROWS, :] = v_ref[...]
    parts = thirds(start_ref[...]) + thirds(dir_ref[...]) + [jnp.zeros((10, LANES), BF16)]
    out_ref[ROWS:, :] = jnp.concatenate(parts, 0)


def project_kernel(steps_ref, own, x1, x3, x2, out_ref, flat):
    refs = (own, x1, x2, x3)
    parts = jnp.concatenate([ref[ROWS:, :] for ref in refs], 1)
    blocks = jnp.concatenate([ref[0:ROWS, :] for ref in refs], 1)
    six = lax.dot_general(
        parts, blocks, (((1,), (1,)), ((), ())), preferred_element_type=F32
    )
    along_start = six[0:1] + six[1:2] + six[2:3]
    along_dir = six[3:4] + six[4:5] + six[5:6]
    for c in range(CHUNKS):
        span = slice(c * LANES, (c + 1) * LANES)
        flat[c : c + 1, :] = along_start[:, span]
        flat[CHUNKS + c : CHUNKS + c + 1, :] = along_dir[:, span]
    squares = jnp.zeros((8, LANES), F32)
    line = lax.broadcasted_iota(jnp.int32, (8, LANES), 0)
    for ref in refs:
        wide = ref[ROWS:, :].astype(F32)
        start = wide[0:1] + wide[1:2] + wide[2:3]
        direction = wide[3:4] + wide[4:5] + wide[5:6]
        squares = squares + jnp.where(line == 0, start * start, 0.0)
        for j in range(3):
            point = start + steps_ref[j] * direction
            squares = squares + jnp.where(line == 1 + j, point * point, 0.0)
    flat[2 * CHUNKS :, :] = squares
    whole = flat[...]
    for i in range(out_ref.shape[0]):
        out_ref[i] = whole


def turn_kernel(own, x1, x3, x2, out_ref):
    def chunk(c, carry):
        span = pl.ds(pl.multiple_of(c * LANES, LANES), LANES)
        for step, ref in enumerate((own, x1, x2, x3)):
            out_ref[step * LANES : (step + 1) * LANES, span] = ref[span, :].T
        return carry

    lax.fori_loop(0, CHUNKS, chunk, 0, unroll=4)


def lane_groups_sum(x, lane):
    for k in (1, 2, 4):
        up = pltpu.roll(x, k, 1)
        down = pltpu.roll(x, LANES - k, 1)
        x = x + jnp.where((lane & k) != 0, up, down)
    return x


def by_row(nominal, counts, lane):
    place = lax.broadcasted_iota(jnp.int32, (CHUNKS, BINS_DEV), 1)
    line = lax.broadcasted_iota(jnp.int32, (CHUNKS, BINS_DEV), 0)
    mine = place // CHUNKS == line
    each = [nominal[p : p + 1] for p in range(PROC)] + [counts]
    spread = jnp.concatenate([jnp.where(mine, row, 0.0) for row in each], 0)
    source = lax.broadcasted_iota(jnp.int32, (BINS_DEV, LANES), 0) % CHUNKS
    target = lax.broadcasted_iota(jnp.int32, (BINS_DEV, LANES), 1) // PROC
    pick = (source == target).astype(F32).astype(BF16)
    high, middle, low = (rows_dot(part, pick) for part in thirds(spread))
    moved = high + middle + low
    out = jnp.zeros((CHUNKS, LANES), F32)
    for p in range(PROC):
        out = jnp.where(lane % PROC == p, moved[p * CHUNKS : (p + 1) * CHUNKS], out)
    return out, moved[PROC * CHUNKS :]


def weights_kernel(got_ref, nominal_ref, counts_ref, steps_ref, v_ref, w_ref, bins_ref, sq_ref):
    total = jnp.sum(got_ref[...], axis=0)
    along_start = total[0:CHUNKS]
    along_dir = total[CHUNKS : 2 * CHUNKS]
    sq_ref[...] = total[2 * CHUNKS : 2 * CHUNKS + 8]
    lane = lax.broadcasted_iota(jnp.int32, (CHUNKS, LANES), 1)
    nominal, counts = by_row(nominal_ref[...], counts_ref[...].astype(F32), lane)
    base = jnp.exp(nominal + along_start)
    base_total = lane_groups_sum(base, lane)
    base_log = jnp.log(base_total)
    part = [None] * 3
    for j in range(3):
        shifted = jnp.exp(nominal + (along_start + steps_ref[j] * along_dir))
        expected = lane_groups_sum(shifted, lane)
        change = (expected - base_total) - counts * (jnp.log(expected) - base_log)
        part[j] = jnp.sum(change, axis=0, keepdims=True) * (1.0 / PROC)
    residual = 1.0 - counts / base_total
    left = residual * base
    w_ref[0] = base
    w_ref[1] = left
    w_ref[2] = (counts / (base_total * base_total)) * base
    grad = jnp.zeros((3, LANES), F32)
    for c in range(CHUNKS):
        row = jnp.concatenate(thirds(left[c : c + 1]), 0)
        grad = grad + rows_dot(row, v_ref[c * LANES : (c + 1) * LANES, :])
    grad = jnp.sum(grad, axis=0, keepdims=True)
    bins_ref[...] = packed(jnp.concatenate([grad] + part, 0))


def hessian_kernel(
    pos_ref, w_ref, extra_ref, turned, own, x1, y1, x3, y3, x2, y2, kept_ref, sent_ref,
    right, jac_rows, jac_cols,
):
    px, py, core = pos_ref[0], pos_ref[1], pos_ref[4]
    mine = lax.broadcasted_iota(jnp.int32, (16, LANES), 1) // PROC
    mine = mine == lax.broadcasted_iota(jnp.int32, (16, LANES), 0)
    down = (own, y1, y2, y3)

    def chunk(c, carry):
        span = pl.ds(pl.multiple_of(c * LANES, LANES), LANES)
        jac_span = pl.ds(pl.multiple_of(c * 16, 16), 16)

        def jacobian(k, refs):
            spread = jnp.where(mine, w_ref[k, pl.ds(c, 1), :], 0.0)
            blocks = jnp.concatenate([ref[span, :] for ref in refs], 1)
            jac = rows_dot(jnp.concatenate(thirds(spread), 0), blocks)
            return (jac[0:16] + jac[16:32] + jac[32:48]).astype(BF16)

        jac_rows[jac_span, :] = jacobian(2, (own, x1, x2, x3))
        jac_cols[jac_span, :] = jacobian(0, down)
        scaled = turned[:, span].astype(F32) * w_ref[1, pl.ds(c, 1), :]
        right[:, span] = scaled.astype(BF16)
        return carry

    lax.fori_loop(0, CHUNKS, chunk, 0, unroll=4)
    right[:, ROWS:] = jac_rows[...].T
    for n in range(2):
        pair = jnp.concatenate([down[2 * n][0:ROWS, :], down[2 * n + 1][0:ROWS, :]], 1)
        both = jnp.concatenate([pair, jac_cols[:, n * 2 * LANES : (n + 1) * 2 * LANES]], 0)
        term = rows_dot(right[...], both)
        for i in range(SIDE):
            row = lax.rem(px + i, SIDE)
            for half in range(2):
                part = term[i * LANES : (i + 1) * LANES, half * LANES : (half + 1) * LANES]
                first, second = part[0:64], part[64:]
                col = lax.rem(py + 2 * n + half, SIDE)
                at = pl.ds(pl.multiple_of((row * SIDE + col) * 64, 64), 64)
                kept_ref[at, :] = jnp.where(core == 0, first, second)
                sent_ref[at, :] = jnp.where(core == 0, second, first).astype(BF16)
    sent_ref[PIECES * 64 :, :] = extra_ref[...]


def pair_kernel(kept_ref, extra_ref, got_ref, out_ref):
    extra = packed(unpacked(extra_ref[...]) + unpacked(got_ref[PIECES * 64 :, :]))
    for k in range(PIECES):
        span = slice(k * 64, (k + 1) * 64)
        both = kept_ref[span, :] + got_ref[span, :].astype(F32)
        out_ref[k, 0:64, :] = both.astype(BF16)
        out_ref[k, 64:, :] = extra


def plane_kernel(pos_ref, got_ref, out_ref):
    py = pos_ref[1]
    extra = unpacked(got_ref[py, 64:, :])
    for k in range(1, SIDE):
        extra = extra + unpacked(got_ref[k * SIDE + py, 64:, :])
    extra = packed(extra)
    for j in range(SIDE):
        tile = got_ref[j, 0:64, :].astype(F32)
        for k in range(1, SIDE):
            tile = tile + got_ref[k * SIDE + j, 0:64, :].astype(F32)
        out_ref[j, 0:64, :] = tile.astype(BF16)
        out_ref[j, 64:, :] = extra


def finish_kernel(pos_ref, got_ref, sq_ref, start_ref, line_ref, grad_ref, hess_ref):
    scale = 1.0 / BIN_TOTAL
    tile = jnp.sum(got_ref[:, 0:64, :].astype(F32), axis=0)
    extra = jnp.sum(unpacked(got_ref[:, 64:, :]), axis=0)
    row = lax.broadcasted_iota(jnp.int32, (64, LANES), 0) + pos_ref[2] * 64
    col = lax.broadcasted_iota(jnp.int32, (64, LANES), 1) + pos_ref[3] * LANES
    hess_ref[...] = (tile + (row == col).astype(F32)) * scale
    grad_ref[...] = (extra[0:1] + start_ref[...]) * scale
    for j in range(3):
        squares = sq_ref[1 + j : 2 + j, :] - sq_ref[0:1, :]
        line_ref[j] = jnp.sum(extra[1 + j : 2 + j, :] + 0.5 * squares) * scale


def arrays_of(*shapes):
    return tuple(jax.ShapeDtypeStruct(s, d) for s, d in shapes)


def from_ahead(array, axis, step):
    return lax.ppermute(array, axis, [((i + step) % SIDE, i) for i in range(SIDE)])


def exchanged(array, axes):
    return lax.all_to_all(array, axes, 0, 0, tiled=True)


def body(log_nominal, variations, observed, start, direction, step_lengths):
    own = variations.reshape(ROWS, LANES)
    packed_own = pl.pallas_call(
        pack_kernel,
        out_shape=jax.ShapeDtypeStruct((ROWS + 16, LANES), BF16),
        in_specs=[VMEM, VMEM, VMEM],
        out_specs=VMEM,
        compiler_params=PARAMS,
        cost_estimate=cost(1_000_000, 1_000_000),
        name="pack",
    )(own, start[None, :], direction[None, :])
    x1, x3, x2 = (from_ahead(packed_own, "x", k) for k in (1, 3, 2))
    y1, y3, y2 = (from_ahead(own, "y", k) for k in (1, 3, 2))
    sent = pl.pallas_call(
        project_kernel,
        out_shape=jax.ShapeDtypeStruct((SIDE, 40, LANES), F32),
        in_specs=[SMEM] + [VMEM] * 4,
        out_specs=VMEM,
        scratch_shapes=[pltpu.VMEM((40, LANES), F32)],
        compiler_params=PARAMS,
        cost_estimate=cost(40_000_000, 2_000_000),
        name="project",
    )(step_lengths, packed_own, x1, x3, x2)
    got = exchanged(sent, "y")
    turned = pl.pallas_call(
        turn_kernel,
        out_shape=jax.ShapeDtypeStruct((SIDE * LANES, ROWS), BF16),
        in_specs=[VMEM] * 4,
        out_specs=VMEM,
        compiler_params=PARAMS,
        cost_estimate=cost(100_000_000, 4_000_000),
        name="turn",
    )(packed_own, x1, x3, x2)
    weights, extra, squares = pl.pallas_call(
        weights_kernel,
        out_shape=arrays_of(
            ((3, CHUNKS, LANES), F32), ((16, LANES), BF16), ((8, LANES), F32)
        ),
        in_specs=[VMEM, VMEM, VMEM, SMEM, VMEM],
        out_specs=(VMEM, VMEM, VMEM),
        compiler_params=PARAMS,
        cost_estimate=cost(10_000_000, 1_000_000),
        name="weights",
    )(got, log_nominal.T, observed[None, :], step_lengths, packed_own)
    px, py = lax.axis_index("x"), lax.axis_index("y")
    core = lax.axis_index("core")
    block = lax.axis_index(("zh", "zl", "core"))
    position = jnp.stack([px, py, block, py * SIDE + px, core]).astype(jnp.int32)
    kept, other = pl.pallas_call(
        hessian_kernel,
        out_shape=arrays_of(
            ((PIECES * 64, LANES), F32), ((PIECES * 64 + 16, LANES), BF16)
        ),
        in_specs=[SMEM] + [VMEM] * 10,
        out_specs=(VMEM, VMEM),
        scratch_shapes=[
            pltpu.VMEM((SIDE * LANES, DEPTH), BF16),
            pltpu.VMEM((BINS_DEV, SIDE * LANES), BF16),
            pltpu.VMEM((BINS_DEV, SIDE * LANES), BF16),
        ],
        compiler_params=PARAMS,
        cost_estimate=cost(2_000_000_000, 5_000_000),
        name="hessian",
    )(position, weights, extra, turned, packed_own, x1, y1, x3, y3, x2, y2)
    swapped = lax.ppermute(other, "core", [(0, 1), (1, 0)])
    pair = pl.pallas_call(
        pair_kernel,
        out_shape=jax.ShapeDtypeStruct((PIECES, 80, LANES), BF16),
        in_specs=[VMEM] * 3,
        out_specs=VMEM,
        compiler_params=PARAMS,
        cost_estimate=cost(1_000_000, 1_000_000),
        name="pair",
    )(kept, extra, swapped)
    near = pl.pallas_call(
        plane_kernel,
        out_shape=jax.ShapeDtypeStruct((SIDE, 80, LANES), BF16),
        in_specs=[SMEM, VMEM],
        out_specs=VMEM,
        compiler_params=PARAMS,
        cost_estimate=cost(1_000_000, 1_000_000),
        name="plane",
    )(position, exchanged(pair, ("zl", "y")))
    line_change, gradient, hessian = pl.pallas_call(
        finish_kernel,
        out_shape=arrays_of(((3,), F32), ((1, LANES), F32), ((64, LANES), F32)),
        in_specs=[SMEM, VMEM, VMEM, VMEM],
        out_specs=(SMEM, VMEM, VMEM),
        compiler_params=PARAMS,
        cost_estimate=cost(1_000_000, 1_000_000),
        name="finish",
    )(position, exchanged(near, "zh"), squares, start[None, :])
    return line_change, gradient[0], hessian


def solution(mesh):
    split = Mesh(
        np.asarray(mesh.devices).reshape(SIDE, SIDE, 2, SIDE, SIDE),
        ("zh", "zl", "core", "y", "x"),
    )
    bins, nuis = ("zh", "zl", "core"), ("y", "x")
    placed = (P(bins, None), P(bins, None, nuis), P(bins), P(nuis), P(nuis), P())
    return jax.shard_map(
        body,
        mesh=split,
        in_specs=placed,
        out_specs=(P(), P(nuis), P(bins, nuis)),
        check_vma=False,
    )
```

```python
import jax
import jax.numpy as jnp
import numpy as np
from jax import lax
from jax.experimental import pallas as pl
from jax.experimental.pallas import tpu as pltpu
from jax.sharding import Mesh
from jax.sharding import PartitionSpec as P


F32 = jnp.float32
BF16 = jnp.bfloat16
SIDE = 4
PROC = 8
ROWS = 2048
BINS_DEV = 256
LANES = 128
CHUNKS = ROWS // LANES
PIECES = SIDE * SIDE
BIN_TOTAL = 32 * BINS_DEV
DEPTH = ROWS + BINS_DEV
VMEM = pl.BlockSpec(memory_space=pltpu.VMEM)
HBM = pl.BlockSpec(memory_space=pltpu.HBM)
SMEM = pl.BlockSpec(memory_space=pltpu.SMEM)
PARAMS = pltpu.CompilerParams(vmem_limit_bytes=12 * 1024 * 1024)


def cost(flops, moved):
    return pl.CostEstimate(flops=flops, bytes_accessed=moved, transcendentals=0)


def thirds(x):
    high = x.astype(BF16)
    rest = x - high.astype(F32)
    middle = rest.astype(BF16)
    low = (rest - middle.astype(F32)).astype(BF16)
    return [high, middle, low]


def rows_dot(a, b):
    return lax.dot_general(a, b, (((1,), (0,)), ((), ())), preferred_element_type=F32)


def packed(four):
    return jnp.concatenate(thirds(four) + [jnp.zeros((4, LANES), BF16)], 0)


def unpacked(rows):
    wide = rows.astype(F32)
    return wide[..., 0:4, :] + wide[..., 4:8, :] + wide[..., 8:12, :]


def project_kernel(v_ref, start_ref, dir_ref, out_ref, flat, rows, ends, sems):
    moves = [
        pltpu.make_async_copy(start_ref, ends.at[0:1], sems.at[0]),
        pltpu.make_async_copy(dir_ref, ends.at[1:2], sems.at[1]),
        pltpu.make_async_copy(v_ref, rows, sems.at[2]),
    ]
    for move in moves:
        move.start()
    for move in moves:
        move.wait()
    start, direction = ends[0:1, :], ends[1:2, :]
    parts = jnp.concatenate(thirds(start) + thirds(direction), 0)
    six = lax.dot_general(
        parts, rows[...], (((1,), (1,)), ((), ())), preferred_element_type=F32
    )
    along_start = six[0:1] + six[1:2] + six[2:3]
    along_dir = six[3:4] + six[4:5] + six[5:6]
    for c in range(CHUNKS):
        span = slice(c * LANES, (c + 1) * LANES)
        flat[c : c + 1, :] = along_start[:, span]
        flat[CHUNKS + c : CHUNKS + c + 1, :] = along_dir[:, span]
    tail = [start * direction, direction * direction, jnp.zeros((6, LANES), F32)]
    flat[2 * CHUNKS :, :] = jnp.concatenate(tail, 0)
    whole = flat[...]
    for i in range(out_ref.shape[0]):
        out_ref[i] = whole


def lane_groups_sum(x, lane):
    for k in (1, 2, 4):
        up = pltpu.roll(x, k, 1)
        down = pltpu.roll(x, LANES - k, 1)
        x = x + jnp.where((lane & k) != 0, up, down)
    return x


def layout_kernel(nominal_ref, counts_ref, steps_ref, out_ref):
    lane = lax.broadcasted_iota(jnp.int32, (CHUNKS, LANES), 1)
    place = lax.broadcasted_iota(jnp.int32, (CHUNKS, BINS_DEV), 1)
    line = lax.broadcasted_iota(jnp.int32, (CHUNKS, BINS_DEV), 0)
    mine = place // CHUNKS == line
    each = [nominal_ref[p : p + 1, :] for p in range(PROC)] + [counts_ref[...].astype(F32)]
    spread = jnp.concatenate([jnp.where(mine, row, 0.0) for row in each], 0)
    source = lax.broadcasted_iota(jnp.int32, (BINS_DEV, LANES), 0) % CHUNKS
    target = lax.broadcasted_iota(jnp.int32, (BINS_DEV, LANES), 1) // PROC
    pick = (source == target).astype(F32).astype(BF16)
    high, middle, low = (rows_dot(part, pick) for part in thirds(spread))
    moved = high + middle + low
    out = jnp.zeros((CHUNKS, LANES), F32)
    for p in range(PROC):
        out = jnp.where(lane % PROC == p, moved[p * CHUNKS : (p + 1) * CHUNKS], out)
    out_ref[0:CHUNKS, :] = out
    out_ref[CHUNKS : 2 * CHUNKS, :] = moved[PROC * CHUNKS :]
    for j in range(3):
        at = 2 * CHUNKS + j
        out_ref[at : at + 1, :] = jnp.full((1, LANES), steps_ref[j], F32)


def weights_kernel(got_ref, local_ref, v_ref, w_ref, bins_ref, sq_ref):
    total = jnp.sum(got_ref[...], axis=0)
    along_start = total[0:CHUNKS]
    along_dir = total[CHUNKS : 2 * CHUNKS]
    cross, square = total[2 * CHUNKS : 2 * CHUNKS + 1], total[2 * CHUNKS + 1 : 2 * CHUNKS + 2]
    lane = lax.broadcasted_iota(jnp.int32, (CHUNKS, LANES), 1)
    nominal, counts = local_ref[0:CHUNKS, :], local_ref[CHUNKS : 2 * CHUNKS, :]
    base = jnp.exp(nominal + along_start)
    base_total = lane_groups_sum(base, lane)
    base_log = jnp.log(base_total)
    part, norms = [], []
    for j in range(3):
        step = local_ref[2 * CHUNKS + j : 2 * CHUNKS + j + 1, :]
        shifted = jnp.exp(nominal + (along_start + step * along_dir))
        expected = lane_groups_sum(shifted, lane)
        change = (expected - base_total) - counts * (jnp.log(expected) - base_log)
        part.append(jnp.sum(change, axis=0, keepdims=True) * (1.0 / PROC))
        norms.append(step * (2.0 * cross + step * square))
    sq_ref[...] = jnp.concatenate(norms + [jnp.zeros((5, LANES), F32)], 0)
    residual = 1.0 - counts / base_total
    left = residual * base
    w_ref[0] = base
    w_ref[1] = left
    w_ref[2] = (counts / (base_total * base_total)) * base
    grad = jnp.zeros((3, LANES), F32)
    for c in range(CHUNKS):
        row = jnp.concatenate(thirds(left[c : c + 1]), 0)
        grad = grad + rows_dot(row, v_ref[c * LANES : (c + 1) * LANES, :])
    grad = jnp.sum(grad, axis=0, keepdims=True)
    bins_ref[...] = packed(jnp.concatenate([grad] + part, 0))


def bin_mask():
    mine = lax.broadcasted_iota(jnp.int32, (16, LANES), 1) // PROC
    return mine == lax.broadcasted_iota(jnp.int32, (16, LANES), 0)


def jacobian(weight, mine, blocks):
    spread = jnp.concatenate(thirds(jnp.where(mine, weight, 0.0)), 0)
    jac = rows_dot(spread, jnp.concatenate(blocks, 1))
    return (jac[0:16] + jac[16:32] + jac[32:48]).astype(BF16)


def rows_kernel(w_ref, own, x1, x3, x2, y3, y2, right, jac_cols, jac_rows):
    mine = bin_mask()

    def chunk(c, carry):
        span = pl.ds(pl.multiple_of(c * LANES, LANES), LANES)
        jac_span = pl.ds(pl.multiple_of(c * 16, 16), 16)
        base, left, curve = (w_ref[k, pl.ds(c, 1), :] for k in range(3))
        across = [ref[span, :] for ref in (own, x1, x2, x3)]
        jac_rows[jac_span, :] = jacobian(curve, mine, across)
        jac_cols[jac_span, :] = jacobian(base, mine, [ref[span, :] for ref in (own, y2, y3)])
        for step, rows in enumerate(across):
            scaled = rows.T.astype(F32) * left
            right[step * LANES : (step + 1) * LANES, span] = scaled.astype(BF16)
        return carry

    lax.fori_loop(0, CHUNKS, chunk, 0, unroll=4)
    right[:, ROWS:] = jac_rows[...].T


def hessian_kernel(
    pos_ref, w_ref, extra_ref, right, jac_ref, own, y2, y3, y1, kept_ref, sent_ref, jac_last
):
    px, py, core = pos_ref[0], pos_ref[1], pos_ref[4]
    mine = bin_mask()
    for c in range(CHUNKS):
        rows = y1[c * LANES : (c + 1) * LANES, :]
        jac_last[c * 16 : (c + 1) * 16, :] = jacobian(w_ref[0, c : c + 1, :], mine, [rows])
    jacs = [jac_ref[:, k * LANES : (k + 1) * LANES] for k in range(3)] + [jac_last[...]]
    steps = ((own, 0), (y2, 2), (y3, 3), (y1, 1))
    for n in range(2):
        cols = [
            jnp.concatenate([steps[k][0][...], jacs[k]], 0) for k in (2 * n, 2 * n + 1)
        ]
        term = rows_dot(right[...], jnp.concatenate(cols, 1))
        for i in range(SIDE):
            row_at = lax.rem(px + i, SIDE)
            for half in range(2):
                part = term[i * LANES : (i + 1) * LANES, half * LANES : (half + 1) * LANES]
                first, second = part[0:64], part[64:]
                col_at = lax.rem(py + steps[2 * n + half][1], SIDE)
                at = pl.ds(pl.multiple_of((row_at * SIDE + col_at) * 64, 64), 64)
                kept_ref[at, :] = jnp.where(core == 0, first, second)
                sent_ref[at, :] = jnp.where(core == 0, second, first).astype(BF16)
    sent_ref[PIECES * 64 :, :] = extra_ref[...]


def pair_kernel(kept_ref, extra_ref, got_ref, out_ref):
    extra = packed(unpacked(extra_ref[...]) + unpacked(got_ref[PIECES * 64 :, :]))
    for k in range(PIECES):
        span = slice(k * 64, (k + 1) * 64)
        both = kept_ref[span, :] + got_ref[span, :].astype(F32)
        out_ref[k, 0:64, :] = both.astype(BF16)
        out_ref[k, 64:, :] = extra


def plane_kernel(pos_ref, got_ref, out_ref):
    py = pos_ref[1]
    extra = unpacked(got_ref[py, 64:, :])
    for k in range(1, SIDE):
        extra = extra + unpacked(got_ref[k * SIDE + py, 64:, :])
    extra = packed(extra)
    for j in range(SIDE):
        tile = got_ref[j, 0:64, :].astype(F32)
        for k in range(1, SIDE):
            tile = tile + got_ref[k * SIDE + j, 0:64, :].astype(F32)
        out_ref[j, 0:64, :] = tile.astype(BF16)
        out_ref[j, 64:, :] = extra


def finish_kernel(pos_ref, got_ref, sq_ref, start_ref, line_ref, grad_ref, hess_ref):
    scale = 1.0 / BIN_TOTAL
    tile = jnp.sum(got_ref[:, 0:64, :].astype(F32), axis=0)
    extra = jnp.sum(unpacked(got_ref[:, 64:, :]), axis=0)
    row = lax.broadcasted_iota(jnp.int32, (64, LANES), 0) + pos_ref[2] * 64
    col = lax.broadcasted_iota(jnp.int32, (64, LANES), 1) + pos_ref[3] * LANES
    hess_ref[...] = (tile + (row == col).astype(F32)) * scale
    grad_ref[...] = (extra[0:1] + start_ref[...]) * scale
    for j in range(3):
        line_ref[j] = jnp.sum(extra[1 + j : 2 + j, :] + 0.5 * sq_ref[j : j + 1, :]) * scale


def arrays_of(*shapes):
    return tuple(jax.ShapeDtypeStruct(s, d) for s, d in shapes)


def from_ahead(array, axis, step):
    return lax.ppermute(array, axis, [((i + step) % SIDE, i) for i in range(SIDE)])


def exchanged(array, axes):
    return lax.all_to_all(array, axes, 0, 0, tiled=True)


def body(log_nominal, variations, observed, start, direction, step_lengths):
    own = variations.reshape(ROWS, LANES)
    sent = pl.pallas_call(
        project_kernel,
        out_shape=jax.ShapeDtypeStruct((16, 40, LANES), F32),
        in_specs=[HBM, HBM, HBM],
        out_specs=VMEM,
        scratch_shapes=[
            pltpu.VMEM((40, LANES), F32),
            pltpu.VMEM((ROWS, LANES), BF16),
            pltpu.VMEM((8, LANES), F32),
            pltpu.SemaphoreType.DMA((3,)),
        ],
        compiler_params=pltpu.CompilerParams(vmem_limit_bytes=62 * 1024 * 1024),
        cost_estimate=cost(10_000_000, 1_000_000),
        name="project",
    )(own, start[None, :], direction[None, :])
    own, sent = lax.optimization_barrier((own, sent))
    x2, y2, x3, y3, x1, y1 = (from_ahead(own, axis, k) for k in (2, 3, 1) for axis in ("x", "y"))
    got = exchanged(sent, ("y", "x"))
    local = pl.pallas_call(
        layout_kernel,
        out_shape=jax.ShapeDtypeStruct((40, LANES), F32),
        in_specs=[VMEM, VMEM, SMEM],
        out_specs=VMEM,
        compiler_params=PARAMS,
        cost_estimate=cost(10_000_000, 1_000_000),
        name="layout",
    )(log_nominal.T, observed[None, :], step_lengths)
    weights, extra, squares = pl.pallas_call(
        weights_kernel,
        out_shape=arrays_of(
            ((3, CHUNKS, LANES), F32), ((16, LANES), BF16), ((8, LANES), F32)
        ),
        in_specs=[VMEM, VMEM, VMEM],
        out_specs=(VMEM, VMEM, VMEM),
        compiler_params=PARAMS,
        cost_estimate=cost(10_000_000, 1_000_000),
        name="weights",
    )(got, local, own)
    px, py = lax.axis_index("x"), lax.axis_index("y")
    core = lax.axis_index("core")
    block = lax.axis_index(("zh", "zl", "core"))
    position = jnp.stack([px, py, block, py * SIDE + px, core]).astype(jnp.int32)
    right, jac_cols = pl.pallas_call(
        rows_kernel,
        out_shape=arrays_of(
            ((SIDE * LANES, DEPTH), BF16), ((BINS_DEV, 3 * LANES), BF16)
        ),
        in_specs=[VMEM] * 7,
        out_specs=(VMEM, VMEM),
        scratch_shapes=[pltpu.VMEM((BINS_DEV, SIDE * LANES), BF16)],
        compiler_params=PARAMS,
        cost_estimate=cost(1_000_000_000, 5_000_000),
        name="rows",
    )(weights, own, x1, x3, x2, y3, y2)
    kept, other = pl.pallas_call(
        hessian_kernel,
        out_shape=arrays_of(
            ((PIECES * 64, LANES), F32), ((PIECES * 64 + 16, LANES), BF16)
        ),
        in_specs=[SMEM] + [VMEM] * 8,
        out_specs=(VMEM, VMEM),
        scratch_shapes=[pltpu.VMEM((BINS_DEV, LANES), BF16)],
        compiler_params=PARAMS,
        cost_estimate=cost(1_000_000_000, 5_000_000),
        name="hessian",
    )(position, weights, extra, right, jac_cols, own, y2, y3, y1)
    swapped = lax.ppermute(other, "core", [(0, 1), (1, 0)])
    pair = pl.pallas_call(
        pair_kernel,
        out_shape=jax.ShapeDtypeStruct((PIECES, 80, LANES), BF16),
        in_specs=[VMEM] * 3,
        out_specs=VMEM,
        compiler_params=PARAMS,
        cost_estimate=cost(1_000_000, 1_000_000),
        name="pair",
    )(kept, extra, swapped)
    near = pl.pallas_call(
        plane_kernel,
        out_shape=jax.ShapeDtypeStruct((SIDE, 80, LANES), BF16),
        in_specs=[SMEM, VMEM],
        out_specs=VMEM,
        compiler_params=PARAMS,
        cost_estimate=cost(1_000_000, 1_000_000),
        name="plane",
    )(position, exchanged(pair, ("zl", "y")))
    line_change, gradient, hessian = pl.pallas_call(
        finish_kernel,
        out_shape=arrays_of(((3,), F32), ((1, LANES), F32), ((64, LANES), F32)),
        in_specs=[SMEM, VMEM, VMEM, VMEM],
        out_specs=(SMEM, VMEM, VMEM),
        compiler_params=PARAMS,
        cost_estimate=cost(1_000_000, 1_000_000),
        name="finish",
    )(position, exchanged(near, "zh"), squares, start[None, :])
    return line_change, gradient[0], hessian


def solution(mesh):
    split = Mesh(
        np.asarray(mesh.devices).reshape(SIDE, SIDE, 2, SIDE, SIDE),
        ("zh", "zl", "core", "y", "x"),
    )
    bins, nuis = ("zh", "zl", "core"), ("y", "x")
    placed = (P(bins, None), P(bins, None, nuis), P(bins), P(nuis), P(nuis), P())
    return jax.shard_map(
        body,
        mesh=split,
        in_specs=placed,
        out_specs=(P(), P(nuis), P(bins, nuis)),
        check_vma=False,
    )
```

```python
import jax
import jax.numpy as jnp
import numpy as np
from jax import lax
from jax.experimental import pallas as pl
from jax.experimental.pallas import tpu as pltpu
from jax.sharding import Mesh
from jax.sharding import PartitionSpec as P


F32 = jnp.float32
BF16 = jnp.bfloat16
SIDE = 4
PROC = 8
ROWS = 2048
BINS_DEV = 256
LANES = 128
CHUNKS = ROWS // LANES
PIECES = SIDE * SIDE
BIN_TOTAL = 32 * BINS_DEV
DEPTH = ROWS + BINS_DEV
VMEM = pl.BlockSpec(memory_space=pltpu.VMEM)
HBM = pl.BlockSpec(memory_space=pltpu.HBM)
SMEM = pl.BlockSpec(memory_space=pltpu.SMEM)
PARAMS = pltpu.CompilerParams(vmem_limit_bytes=12 * 1024 * 1024)


def cost(flops, moved):
    return pl.CostEstimate(flops=flops, bytes_accessed=moved, transcendentals=0)


def thirds(x):
    high = x.astype(BF16)
    rest = x - high.astype(F32)
    middle = rest.astype(BF16)
    low = (rest - middle.astype(F32)).astype(BF16)
    return [high, middle, low]


def rows_dot(a, b):
    return lax.dot_general(a, b, (((1,), (0,)), ((), ())), preferred_element_type=F32)


def packed(four):
    return jnp.concatenate(thirds(four) + [jnp.zeros((4, LANES), BF16)], 0)


def unpacked(rows):
    wide = rows.astype(F32)
    return wide[..., 0:4, :] + wide[..., 4:8, :] + wide[..., 8:12, :]


def project_kernel(v_ref, start_ref, dir_ref, out_ref, flat, rows, ends, sems):
    moves = [
        pltpu.make_async_copy(start_ref, ends.at[0:1], sems.at[0]),
        pltpu.make_async_copy(dir_ref, ends.at[1:2], sems.at[1]),
        pltpu.make_async_copy(v_ref, rows, sems.at[2]),
    ]
    for move in moves:
        move.start()
    for move in moves:
        move.wait()
    start, direction = ends[0:1, :], ends[1:2, :]
    parts = jnp.concatenate(thirds(start) + thirds(direction), 0)
    six = lax.dot_general(
        parts, rows[...], (((1,), (1,)), ((), ())), preferred_element_type=F32
    )
    along_start = six[0:1] + six[1:2] + six[2:3]
    along_dir = six[3:4] + six[4:5] + six[5:6]
    for c in range(CHUNKS):
        span = slice(c * LANES, (c + 1) * LANES)
        flat[c : c + 1, :] = along_start[:, span]
        flat[CHUNKS + c : CHUNKS + c + 1, :] = along_dir[:, span]
    tail = [start * direction, direction * direction, jnp.zeros((6, LANES), F32)]
    flat[2 * CHUNKS :, :] = jnp.concatenate(tail, 0)
    whole = flat[...]
    for i in range(out_ref.shape[0]):
        out_ref[i] = whole


def lane_groups_sum(x, lane):
    for k in (1, 2, 4):
        up = pltpu.roll(x, k, 1)
        down = pltpu.roll(x, LANES - k, 1)
        x = x + jnp.where((lane & k) != 0, up, down)
    return x


def layout_kernel(nominal_ref, counts_ref, steps_ref, own_ref, out_ref, near_ref):
    near_ref[...] = own_ref[...]
    lane = lax.broadcasted_iota(jnp.int32, (CHUNKS, LANES), 1)
    place = lax.broadcasted_iota(jnp.int32, (CHUNKS, BINS_DEV), 1)
    line = lax.broadcasted_iota(jnp.int32, (CHUNKS, BINS_DEV), 0)
    mine = place // CHUNKS == line
    each = [nominal_ref[p : p + 1, :] for p in range(PROC)] + [counts_ref[...].astype(F32)]
    spread = jnp.concatenate([jnp.where(mine, row, 0.0) for row in each], 0)
    source = lax.broadcasted_iota(jnp.int32, (BINS_DEV, LANES), 0) % CHUNKS
    target = lax.broadcasted_iota(jnp.int32, (BINS_DEV, LANES), 1) // PROC
    pick = (source == target).astype(F32).astype(BF16)
    high, middle, low = (rows_dot(part, pick) for part in thirds(spread))
    moved = high + middle + low
    out = jnp.zeros((CHUNKS, LANES), F32)
    for p in range(PROC):
        out = jnp.where(lane % PROC == p, moved[p * CHUNKS : (p + 1) * CHUNKS], out)
    out_ref[0:CHUNKS, :] = out
    out_ref[CHUNKS : 2 * CHUNKS, :] = moved[PROC * CHUNKS :]
    for j in range(3):
        at = 2 * CHUNKS + j
        out_ref[at : at + 1, :] = jnp.full((1, LANES), steps_ref[j], F32)


def weights_kernel(got_ref, local_ref, w_ref, change_ref, sq_ref):
    total = jnp.sum(got_ref[...], axis=0)
    along_start = total[0:CHUNKS]
    along_dir = total[CHUNKS : 2 * CHUNKS]
    cross, square = total[2 * CHUNKS : 2 * CHUNKS + 1], total[2 * CHUNKS + 1 : 2 * CHUNKS + 2]
    lane = lax.broadcasted_iota(jnp.int32, (CHUNKS, LANES), 1)
    nominal, counts = local_ref[0:CHUNKS, :], local_ref[CHUNKS : 2 * CHUNKS, :]
    base = jnp.exp(nominal + along_start)
    base_total = lane_groups_sum(base, lane)
    base_log = jnp.log(base_total)
    part, norms = [], []
    for j in range(3):
        step = local_ref[2 * CHUNKS + j : 2 * CHUNKS + j + 1, :]
        shifted = jnp.exp(nominal + (along_start + step * along_dir))
        expected = lane_groups_sum(shifted, lane)
        change = (expected - base_total) - counts * (jnp.log(expected) - base_log)
        part.append(jnp.sum(change, axis=0, keepdims=True) * (1.0 / PROC))
        norms.append(step * (2.0 * cross + step * square))
    sq_ref[...] = jnp.concatenate(norms + [jnp.zeros((5, LANES), F32)], 0)
    residual = 1.0 - counts / base_total
    left = residual * base
    w_ref[0] = base
    w_ref[1] = left
    w_ref[2] = (counts / (base_total * base_total)) * base
    change_ref[...] = jnp.concatenate(part + [jnp.zeros((5, LANES), F32)], 0)


def bin_mask():
    mine = lax.broadcasted_iota(jnp.int32, (16, LANES), 1) // PROC
    return mine == lax.broadcasted_iota(jnp.int32, (16, LANES), 0)


def jacobian(weight, mine, blocks):
    spread = jnp.concatenate(thirds(jnp.where(mine, weight, 0.0)), 0)
    jac = rows_dot(spread, jnp.concatenate(blocks, 1))
    return (jac[0:16] + jac[16:32] + jac[32:48]).astype(BF16)


def rows_kernel(
    w_ref, change_ref, own, x1, x3, x2, y3, y2, right, jac_cols, extra_ref, jac_rows, grad
):
    mine = bin_mask()
    grad[...] = jnp.zeros((LANES, LANES), F32)

    def chunk(c, carry):
        span = pl.ds(pl.multiple_of(c * LANES, LANES), LANES)
        jac_span = pl.ds(pl.multiple_of(c * 16, 16), 16)
        base, left, curve = (w_ref[k, pl.ds(c, 1), :] for k in range(3))
        across = [ref[span, :] for ref in (own, x1, x2, x3)]
        jac_rows[jac_span, :] = jacobian(curve, mine, across)
        jac_cols[jac_span, :] = jacobian(base, mine, [ref[span, :] for ref in (own, y2, y3)])
        for step, rows in enumerate(across):
            scaled = rows.T.astype(F32) * left
            if step == 0:
                grad[...] += scaled
            right[step * LANES : (step + 1) * LANES, span] = scaled.astype(BF16)
        return carry

    lax.fori_loop(0, CHUNKS, chunk, 0, unroll=4)
    right[:, ROWS:] = jac_rows[...].T
    total = jnp.sum(grad[...].T, axis=0, keepdims=True)
    extra_ref[...] = packed(jnp.concatenate([total, change_ref[0:3, :]], 0))


def hessian_kernel(
    pos_ref, w_ref, extra_ref, right, jac_ref, own, y2, y3, y1, kept_ref, sent_ref, jac_last
):
    px, py, core = pos_ref[0], pos_ref[1], pos_ref[4]
    mine = bin_mask()
    for c in range(CHUNKS):
        rows = y1[c * LANES : (c + 1) * LANES, :]
        jac_last[c * 16 : (c + 1) * 16, :] = jacobian(w_ref[0, c : c + 1, :], mine, [rows])
    jacs = [jac_ref[:, k * LANES : (k + 1) * LANES] for k in range(3)] + [jac_last[...]]
    steps = ((own, 0), (y2, 2), (y3, 3), (y1, 1))
    for n in range(2):
        cols = [
            jnp.concatenate([steps[k][0][...], jacs[k]], 0) for k in (2 * n, 2 * n + 1)
        ]
        term = rows_dot(right[...], jnp.concatenate(cols, 1))
        for i in range(SIDE):
            row_at = lax.rem(px + i, SIDE)
            for half in range(2):
                part = term[i * LANES : (i + 1) * LANES, half * LANES : (half + 1) * LANES]
                first, second = part[0:64], part[64:]
                col_at = lax.rem(py + steps[2 * n + half][1], SIDE)
                at = pl.ds(pl.multiple_of((row_at * SIDE + col_at) * 64, 64), 64)
                kept_ref[at, :] = jnp.where(core == 0, first, second)
                sent_ref[at, :] = jnp.where(core == 0, second, first).astype(BF16)
    sent_ref[PIECES * 64 :, :] = extra_ref[...]


def pair_kernel(kept_ref, extra_ref, got_ref, out_ref):
    extra = packed(unpacked(extra_ref[...]) + unpacked(got_ref[PIECES * 64 :, :]))
    for k in range(PIECES):
        span = slice(k * 64, (k + 1) * 64)
        both = kept_ref[span, :] + got_ref[span, :].astype(F32)
        out_ref[k, 0:64, :] = both.astype(BF16)
        out_ref[k, 64:, :] = extra


def plane_kernel(pos_ref, got_ref, out_ref):
    py = pos_ref[1]
    extra = unpacked(got_ref[py, 64:, :])
    for k in range(1, SIDE):
        extra = extra + unpacked(got_ref[k * SIDE + py, 64:, :])
    extra = packed(extra)
    for j in range(SIDE):
        tile = got_ref[j, 0:64, :].astype(F32)
        for k in range(1, SIDE):
            tile = tile + got_ref[k * SIDE + j, 0:64, :].astype(F32)
        out_ref[j, 0:64, :] = tile.astype(BF16)
        out_ref[j, 64:, :] = extra


def finish_kernel(pos_ref, got_ref, sq_ref, start_ref, line_ref, grad_ref, hess_ref):
    scale = 1.0 / BIN_TOTAL
    tile = jnp.sum(got_ref[:, 0:64, :].astype(F32), axis=0)
    extra = jnp.sum(unpacked(got_ref[:, 64:, :]), axis=0)
    row = lax.broadcasted_iota(jnp.int32, (64, LANES), 0) + pos_ref[2] * 64
    col = lax.broadcasted_iota(jnp.int32, (64, LANES), 1) + pos_ref[3] * LANES
    hess_ref[...] = (tile + (row == col).astype(F32)) * scale
    grad_ref[...] = (extra[0:1] + start_ref[...]) * scale
    for j in range(3):
        line_ref[j] = jnp.sum(extra[1 + j : 2 + j, :] + 0.5 * sq_ref[j : j + 1, :]) * scale


def arrays_of(*shapes):
    return tuple(jax.ShapeDtypeStruct(s, d) for s, d in shapes)


def from_ahead(array, axis, step):
    return lax.ppermute(array, axis, [((i + step) % SIDE, i) for i in range(SIDE)])


def exchanged(array, axes):
    return lax.all_to_all(array, axes, 0, 0, tiled=True)


def body(log_nominal, variations, observed, start, direction, step_lengths):
    own = variations.reshape(ROWS, LANES)
    sent = pl.pallas_call(
        project_kernel,
        out_shape=jax.ShapeDtypeStruct((16, 40, LANES), F32),
        in_specs=[HBM, HBM, HBM],
        out_specs=VMEM,
        scratch_shapes=[
            pltpu.VMEM((40, LANES), F32),
            pltpu.VMEM((ROWS, LANES), BF16),
            pltpu.VMEM((8, LANES), F32),
            pltpu.SemaphoreType.DMA((3,)),
        ],
        compiler_params=pltpu.CompilerParams(vmem_limit_bytes=62 * 1024 * 1024),
        cost_estimate=cost(10_000_000, 1_000_000),
        name="project",
    )(own, start[None, :], direction[None, :])
    own, sent = lax.optimization_barrier((own, sent))
    x2, y2, x3, y3, x1, y1 = (from_ahead(own, axis, k) for k in (2, 3, 1) for axis in ("x", "y"))
    got = exchanged(sent, ("y", "x"))
    local, near_own = pl.pallas_call(
        layout_kernel,
        out_shape=arrays_of(((40, LANES), F32), ((ROWS, LANES), BF16)),
        in_specs=[VMEM, VMEM, SMEM, VMEM],
        out_specs=(VMEM, VMEM),
        compiler_params=PARAMS,
        cost_estimate=cost(10_000_000, 1_000_000),
        name="layout",
    )(log_nominal.T, observed[None, :], step_lengths, own)
    weights, changes, squares = pl.pallas_call(
        weights_kernel,
        out_shape=arrays_of(
            ((3, CHUNKS, LANES), F32), ((8, LANES), F32), ((8, LANES), F32)
        ),
        in_specs=[VMEM, VMEM],
        out_specs=(VMEM, VMEM, VMEM),
        compiler_params=PARAMS,
        cost_estimate=cost(10_000_000, 1_000_000),
        name="weights",
    )(got, local)
    px, py = lax.axis_index("x"), lax.axis_index("y")
    core = lax.axis_index("core")
    block = lax.axis_index(("zh", "zl", "core"))
    position = jnp.stack([px, py, block, py * SIDE + px, core]).astype(jnp.int32)
    right, jac_cols, extra = pl.pallas_call(
        rows_kernel,
        out_shape=arrays_of(
            ((SIDE * LANES, DEPTH), BF16), ((BINS_DEV, 3 * LANES), BF16), ((16, LANES), BF16)
        ),
        in_specs=[VMEM] * 8,
        out_specs=(VMEM, VMEM, VMEM),
        scratch_shapes=[
            pltpu.VMEM((BINS_DEV, SIDE * LANES), BF16),
            pltpu.VMEM((LANES, LANES), F32),
        ],
        compiler_params=PARAMS,
        cost_estimate=cost(1_000_000_000, 5_000_000),
        name="rows",
    )(weights, changes, near_own, x1, x3, x2, y3, y2)
    kept, other = pl.pallas_call(
        hessian_kernel,
        out_shape=arrays_of(
            ((PIECES * 64, LANES), F32), ((PIECES * 64 + 16, LANES), BF16)
        ),
        in_specs=[SMEM] + [VMEM] * 8,
        out_specs=(VMEM, VMEM),
        scratch_shapes=[pltpu.VMEM((BINS_DEV, LANES), BF16)],
        compiler_params=PARAMS,
        cost_estimate=cost(1_000_000_000, 5_000_000),
        name="hessian",
    )(position, weights, extra, right, jac_cols, near_own, y2, y3, y1)
    swapped = lax.ppermute(other, "core", [(0, 1), (1, 0)])
    pair = pl.pallas_call(
        pair_kernel,
        out_shape=jax.ShapeDtypeStruct((PIECES, 80, LANES), BF16),
        in_specs=[VMEM] * 3,
        out_specs=VMEM,
        compiler_params=PARAMS,
        cost_estimate=cost(1_000_000, 1_000_000),
        name="pair",
    )(kept, extra, swapped)
    near = pl.pallas_call(
        plane_kernel,
        out_shape=jax.ShapeDtypeStruct((SIDE, 80, LANES), BF16),
        in_specs=[SMEM, VMEM],
        out_specs=VMEM,
        compiler_params=PARAMS,
        cost_estimate=cost(1_000_000, 1_000_000),
        name="plane",
    )(position, exchanged(pair, ("zl", "y")))
    line_change, gradient, hessian = pl.pallas_call(
        finish_kernel,
        out_shape=arrays_of(((3,), F32), ((1, LANES), F32), ((64, LANES), F32)),
        in_specs=[SMEM, VMEM, VMEM, VMEM],
        out_specs=(SMEM, VMEM, VMEM),
        compiler_params=PARAMS,
        cost_estimate=cost(1_000_000, 1_000_000),
        name="finish",
    )(position, exchanged(near, "zh"), squares, start[None, :])
    return line_change, gradient[0], hessian


def solution(mesh):
    split = Mesh(
        np.asarray(mesh.devices).reshape(SIDE, SIDE, 2, SIDE, SIDE),
        ("zh", "zl", "core", "y", "x"),
    )
    bins, nuis = ("zh", "zl", "core"), ("y", "x")
    placed = (P(bins, None), P(bins, None, nuis), P(bins), P(nuis), P(nuis), P())
    return jax.shard_map(
        body,
        mesh=split,
        in_specs=placed,
        out_specs=(P(), P(nuis), P(bins, nuis)),
        check_vma=False,
    )
```

```python
import jax
import jax.numpy as jnp
import numpy as np
from jax import lax
from jax.experimental import pallas as pl
from jax.experimental.pallas import tpu as pltpu
from jax.sharding import Mesh
from jax.sharding import PartitionSpec as P


F32 = jnp.float32
BF16 = jnp.bfloat16
SIDE = 4
PROC = 8
ROWS = 2048
BINS_DEV = 256
LANES = 128
CHUNKS = ROWS // LANES
PIECES = SIDE * SIDE
BIN_TOTAL = 32 * BINS_DEV
DEPTH = ROWS + BINS_DEV
VMEM = pl.BlockSpec(memory_space=pltpu.VMEM)
HBM = pl.BlockSpec(memory_space=pltpu.HBM)
SMEM = pl.BlockSpec(memory_space=pltpu.SMEM)
PARAMS = pltpu.CompilerParams(vmem_limit_bytes=12 * 1024 * 1024)


def cost(flops, moved):
    return pl.CostEstimate(flops=flops, bytes_accessed=moved, transcendentals=0)


def thirds(x):
    high = x.astype(BF16)
    rest = x - high.astype(F32)
    middle = rest.astype(BF16)
    low = (rest - middle.astype(F32)).astype(BF16)
    return [high, middle, low]


def rows_dot(a, b):
    return lax.dot_general(a, b, (((1,), (0,)), ((), ())), preferred_element_type=F32)


def packed(four):
    return jnp.concatenate(thirds(four) + [jnp.zeros((4, LANES), BF16)], 0)


def unpacked(rows):
    wide = rows.astype(F32)
    return wide[..., 0:4, :] + wide[..., 4:8, :] + wide[..., 8:12, :]


def project_kernel(v_ref, start_ref, dir_ref, out_ref, rows, flat, ends, sems):
    moves = [
        pltpu.make_async_copy(start_ref, ends.at[0:1], sems.at[0]),
        pltpu.make_async_copy(dir_ref, ends.at[1:2], sems.at[1]),
        pltpu.make_async_copy(v_ref, rows, sems.at[2]),
    ]
    for move in moves:
        move.start()
    for move in moves:
        move.wait()
    start, direction = ends[0:1, :], ends[1:2, :]
    parts = jnp.concatenate(thirds(start) + thirds(direction), 0)
    six = lax.dot_general(
        parts, rows[...], (((1,), (1,)), ((), ())), preferred_element_type=F32
    )
    along_start = six[0:1] + six[1:2] + six[2:3]
    along_dir = six[3:4] + six[4:5] + six[5:6]
    for c in range(CHUNKS):
        span = slice(c * LANES, (c + 1) * LANES)
        flat[c : c + 1, :] = along_start[:, span]
        flat[CHUNKS + c : CHUNKS + c + 1, :] = along_dir[:, span]
    tail = [start * direction, direction * direction, jnp.zeros((6, LANES), F32)]
    flat[2 * CHUNKS :, :] = jnp.concatenate(tail, 0)
    whole = flat[...]
    for i in range(out_ref.shape[0]):
        out_ref[i] = whole


def lane_groups_sum(x, lane):
    for k in (1, 2, 4):
        up = pltpu.roll(x, k, 1)
        down = pltpu.roll(x, LANES - k, 1)
        x = x + jnp.where((lane & k) != 0, up, down)
    return x


def layout_kernel(nominal_ref, counts_ref, steps_ref, out_ref):
    lane = lax.broadcasted_iota(jnp.int32, (CHUNKS, LANES), 1)
    place = lax.broadcasted_iota(jnp.int32, (CHUNKS, BINS_DEV), 1)
    line = lax.broadcasted_iota(jnp.int32, (CHUNKS, BINS_DEV), 0)
    mine = place // CHUNKS == line
    each = [nominal_ref[p : p + 1, :] for p in range(PROC)] + [counts_ref[...].astype(F32)]
    spread = jnp.concatenate([jnp.where(mine, row, 0.0) for row in each], 0)
    source = lax.broadcasted_iota(jnp.int32, (BINS_DEV, LANES), 0) % CHUNKS
    target = lax.broadcasted_iota(jnp.int32, (BINS_DEV, LANES), 1) // PROC
    pick = (source == target).astype(F32).astype(BF16)
    high, middle, low = (rows_dot(part, pick) for part in thirds(spread))
    moved = high + middle + low
    out = jnp.zeros((CHUNKS, LANES), F32)
    for p in range(PROC):
        out = jnp.where(lane % PROC == p, moved[p * CHUNKS : (p + 1) * CHUNKS], out)
    out_ref[0:CHUNKS, :] = out
    out_ref[CHUNKS : 2 * CHUNKS, :] = moved[PROC * CHUNKS :]
    for j in range(3):
        at = 2 * CHUNKS + j
        out_ref[at : at + 1, :] = jnp.full((1, LANES), steps_ref[j], F32)


def weights_kernel(got_ref, local_ref, w_ref, change_ref, sq_ref):
    total = jnp.sum(got_ref[...], axis=0)
    along_start = total[0:CHUNKS]
    along_dir = total[CHUNKS : 2 * CHUNKS]
    cross, square = total[2 * CHUNKS : 2 * CHUNKS + 1], total[2 * CHUNKS + 1 : 2 * CHUNKS + 2]
    lane = lax.broadcasted_iota(jnp.int32, (CHUNKS, LANES), 1)
    nominal, counts = local_ref[0:CHUNKS, :], local_ref[CHUNKS : 2 * CHUNKS, :]
    base = jnp.exp(nominal + along_start)
    base_total = lane_groups_sum(base, lane)
    base_log = jnp.log(base_total)
    part, norms = [], []
    for j in range(3):
        step = local_ref[2 * CHUNKS + j : 2 * CHUNKS + j + 1, :]
        shifted = jnp.exp(nominal + (along_start + step * along_dir))
        expected = lane_groups_sum(shifted, lane)
        change = (expected - base_total) - counts * (jnp.log(expected) - base_log)
        part.append(jnp.sum(change, axis=0, keepdims=True) * (1.0 / PROC))
        norms.append(step * (2.0 * cross + step * square))
    sq_ref[...] = jnp.concatenate(norms + [jnp.zeros((5, LANES), F32)], 0)
    residual = 1.0 - counts / base_total
    left = residual * base
    w_ref[0] = base
    w_ref[1] = left
    w_ref[2] = (counts / (base_total * base_total)) * base
    change_ref[...] = jnp.concatenate(part + [jnp.zeros((5, LANES), F32)], 0)


def bin_mask():
    mine = lax.broadcasted_iota(jnp.int32, (16, LANES), 1) // PROC
    return mine == lax.broadcasted_iota(jnp.int32, (16, LANES), 0)


def jacobian(weight, mine, blocks):
    spread = jnp.concatenate(thirds(jnp.where(mine, weight, 0.0)), 0)
    jac = rows_dot(spread, jnp.concatenate(blocks, 1))
    return (jac[0:16] + jac[16:32] + jac[32:48]).astype(BF16)


def rows_kernel(
    w_ref, change_ref, own, xa, xb, xr, ya, right, jac_cols, extra_ref, jac_rows, grad
):
    mine = bin_mask()
    grad[...] = jnp.zeros((LANES, LANES), F32)

    def chunk(c, carry):
        span = pl.ds(pl.multiple_of(c * LANES, LANES), LANES)
        jac_span = pl.ds(pl.multiple_of(c * 16, 16), 16)
        base, left, curve = (w_ref[k, pl.ds(c, 1), :] for k in range(3))
        across = [ref[span, :] for ref in (own, xa, xb, xr)]
        jac_rows[jac_span, :] = jacobian(curve, mine, across)
        jac_cols[jac_span, :] = jacobian(base, mine, [ref[span, :] for ref in (own, ya)])
        for step, rows in enumerate(across):
            scaled = rows.T.astype(F32) * left
            if step == 0:
                grad[...] += scaled
            right[step * LANES : (step + 1) * LANES, span] = scaled.astype(BF16)
        return carry

    lax.fori_loop(0, CHUNKS, chunk, 0, unroll=4)
    right[:, ROWS:] = jac_rows[...].T
    total = jnp.sum(grad[...].T, axis=0, keepdims=True)
    extra_ref[...] = packed(jnp.concatenate([total, change_ref[0:3, :]], 0))


def hessian_kernel(
    pos_ref, w_ref, extra_ref, right, jac_ref, own, ya, yb, yr, kept_ref, sent_ref, jac_last
):
    px, py, core = pos_ref[0], pos_ref[1], pos_ref[4]
    mine = bin_mask()
    for c in range(CHUNKS):
        rows = [ref[c * LANES : (c + 1) * LANES, :] for ref in (yb, yr)]
        jac_last[c * 16 : (c + 1) * 16, :] = jacobian(w_ref[0, c : c + 1, :], mine, rows)
    jacs = [ref[:, k * LANES : (k + 1) * LANES] for ref in (jac_ref, jac_last) for k in range(2)]
    steps = (0, 1 + 2 * core, 3 - 2 * core, 2)
    cols_in = (own, ya, yb, yr)
    for n in range(2):
        cols = [
            jnp.concatenate([cols_in[k][...], jacs[k]], 0) for k in (2 * n, 2 * n + 1)
        ]
        term = rows_dot(right[...], jnp.concatenate(cols, 1))
        for i in range(SIDE):
            row_at = lax.rem(px + steps[i], SIDE)
            for half in range(2):
                part = term[i * LANES : (i + 1) * LANES, half * LANES : (half + 1) * LANES]
                first, second = part[0:64], part[64:]
                col_at = lax.rem(py + steps[2 * n + half], SIDE)
                at = pl.ds(pl.multiple_of((row_at * SIDE + col_at) * 64, 64), 64)
                kept_ref[at, :] = jnp.where(core == 0, first, second)
                sent_ref[at, :] = jnp.where(core == 0, second, first).astype(BF16)
    sent_ref[PIECES * 64 :, :] = extra_ref[...]


def pair_kernel(kept_ref, extra_ref, got_ref, out_ref):
    extra = packed(unpacked(extra_ref[...]) + unpacked(got_ref[PIECES * 64 :, :]))
    for k in range(PIECES):
        span = slice(k * 64, (k + 1) * 64)
        both = kept_ref[span, :] + got_ref[span, :].astype(F32)
        out_ref[k, 0:64, :] = both.astype(BF16)
        out_ref[k, 64:, :] = extra


def plane_kernel(pos_ref, got_ref, out_ref):
    py = pos_ref[1]
    extra = unpacked(got_ref[py, 64:, :])
    for k in range(1, SIDE):
        extra = extra + unpacked(got_ref[k * SIDE + py, 64:, :])
    extra = packed(extra)
    for j in range(SIDE):
        tile = got_ref[j, 0:64, :].astype(F32)
        for k in range(1, SIDE):
            tile = tile + got_ref[k * SIDE + j, 0:64, :].astype(F32)
        out_ref[j, 0:64, :] = tile.astype(BF16)
        out_ref[j, 64:, :] = extra


def finish_kernel(pos_ref, got_ref, sq_ref, start_ref, line_ref, grad_ref, hess_ref):
    scale = 1.0 / BIN_TOTAL
    tile = jnp.sum(got_ref[:, 0:64, :].astype(F32), axis=0)
    extra = jnp.sum(unpacked(got_ref[:, 64:, :]), axis=0)
    row = lax.broadcasted_iota(jnp.int32, (64, LANES), 0) + pos_ref[2] * 64
    col = lax.broadcasted_iota(jnp.int32, (64, LANES), 1) + pos_ref[3] * LANES
    hess_ref[...] = (tile + (row == col).astype(F32)) * scale
    grad_ref[...] = (extra[0:1] + start_ref[...]) * scale
    for j in range(3):
        line_ref[j] = jnp.sum(extra[1 + j : 2 + j, :] + 0.5 * sq_ref[j : j + 1, :]) * scale


def in_hbm(array):
    return pltpu.with_memory_space_constraint(array, pltpu.HBM)


def arrays_of(*shapes):
    return tuple(jax.ShapeDtypeStruct(s, d) for s, d in shapes)


def around(array, axis, way):
    pairs = []
    for core in range(2):
        step = way if core == 0 else -way
        pairs += [(core * SIDE + (i + step) % SIDE, core * SIDE + i) for i in range(SIDE)]
    return lax.ppermute(array, ("core", axis), pairs)


def exchanged(array, axes):
    return lax.all_to_all(array, axes, 0, 0, tiled=True)


def body(log_nominal, variations, observed, start, direction, step_lengths):
    own = variations.reshape(ROWS, LANES)
    sent, own = pl.pallas_call(
        project_kernel,
        out_shape=arrays_of(((16, 40, LANES), F32), ((ROWS, LANES), BF16)),
        in_specs=[HBM, HBM, HBM],
        out_specs=(VMEM, VMEM),
        scratch_shapes=[
            pltpu.VMEM((40, LANES), F32),
            pltpu.VMEM((8, LANES), F32),
            pltpu.SemaphoreType.DMA((3,)),
        ],
        compiler_params=PARAMS,
        cost_estimate=cost(10_000_000, 1_000_000),
        name="project",
    )(in_hbm(own), in_hbm(start[None, :]), in_hbm(direction[None, :]))
    xa, ya = (around(own, axis, 1) for axis in ("x", "y"))
    xb, yb = (around(own, axis, -1) for axis in ("x", "y"))
    xr, yr = (around(got, axis, 1) for got, axis in ((xa, "x"), (ya, "y")))
    got = exchanged(sent, ("y", "x"))
    local = pl.pallas_call(
        layout_kernel,
        out_shape=jax.ShapeDtypeStruct((40, LANES), F32),
        in_specs=[VMEM, VMEM, SMEM],
        out_specs=VMEM,
        compiler_params=PARAMS,
        cost_estimate=cost(10_000_000, 1_000_000),
        name="layout",
    )(*map(in_hbm, (log_nominal.T, observed[None, :], step_lengths)))
    weights, changes, squares = pl.pallas_call(
        weights_kernel,
        out_shape=arrays_of(
            ((3, CHUNKS, LANES), F32), ((8, LANES), F32), ((8, LANES), F32)
        ),
        in_specs=[VMEM, VMEM],
        out_specs=(VMEM, VMEM, VMEM),
        compiler_params=PARAMS,
        cost_estimate=cost(10_000_000, 1_000_000),
        name="weights",
    )(got, local)
    px, py = lax.axis_index("x"), lax.axis_index("y")
    core = lax.axis_index("core")
    block = lax.axis_index(("zh", "zl", "core"))
    position = jnp.stack([px, py, block, py * SIDE + px, core]).astype(jnp.int32)
    right, jac_cols, extra = pl.pallas_call(
        rows_kernel,
        out_shape=arrays_of(
            ((SIDE * LANES, DEPTH), BF16), ((BINS_DEV, 2 * LANES), BF16), ((16, LANES), BF16)
        ),
        in_specs=[VMEM] * 7,
        out_specs=(VMEM, VMEM, VMEM),
        scratch_shapes=[
            pltpu.VMEM((BINS_DEV, SIDE * LANES), BF16),
            pltpu.VMEM((LANES, LANES), F32),
        ],
        compiler_params=PARAMS,
        cost_estimate=cost(1_000_000_000, 5_000_000),
        name="rows",
    )(weights, changes, own, xa, xb, xr, ya)
    kept, other = pl.pallas_call(
        hessian_kernel,
        out_shape=arrays_of(
            ((PIECES * 64, LANES), F32), ((PIECES * 64 + 16, LANES), BF16)
        ),
        in_specs=[SMEM] + [VMEM] * 8,
        out_specs=(VMEM, VMEM),
        scratch_shapes=[pltpu.VMEM((BINS_DEV, 2 * LANES), BF16)],
        compiler_params=PARAMS,
        cost_estimate=cost(1_000_000_000, 5_000_000),
        name="hessian",
    )(position, weights, extra, right, jac_cols, own, ya, yb, yr)
    swapped = lax.ppermute(other, "core", [(0, 1), (1, 0)])
    pair = pl.pallas_call(
        pair_kernel,
        out_shape=jax.ShapeDtypeStruct((PIECES, 80, LANES), BF16),
        in_specs=[VMEM] * 3,
        out_specs=VMEM,
        compiler_params=PARAMS,
        cost_estimate=cost(1_000_000, 1_000_000),
        name="pair",
    )(kept, extra, swapped)
    near = pl.pallas_call(
        plane_kernel,
        out_shape=jax.ShapeDtypeStruct((SIDE, 80, LANES), BF16),
        in_specs=[SMEM, VMEM],
        out_specs=VMEM,
        compiler_params=PARAMS,
        cost_estimate=cost(1_000_000, 1_000_000),
        name="plane",
    )(position, exchanged(pair, ("zl", "y")))
    line_change, gradient, hessian = pl.pallas_call(
        finish_kernel,
        out_shape=arrays_of(((3,), F32), ((1, LANES), F32), ((64, LANES), F32)),
        in_specs=[SMEM, VMEM, VMEM, VMEM],
        out_specs=(SMEM, VMEM, VMEM),
        compiler_params=PARAMS,
        cost_estimate=cost(1_000_000, 1_000_000),
        name="finish",
    )(position, exchanged(near, "zh"), squares, start[None, :])
    return line_change, gradient[0], hessian


def solution(mesh):
    split = Mesh(
        np.asarray(mesh.devices).reshape(SIDE, SIDE, 2, SIDE, SIDE),
        ("zh", "zl", "core", "y", "x"),
    )
    bins, nuis = ("zh", "zl", "core"), ("y", "x")
    placed = (P(bins, None), P(bins, None, nuis), P(bins), P(nuis), P(nuis), P())
    return jax.shard_map(
        body,
        mesh=split,
        in_specs=placed,
        out_specs=(P(), P(nuis), P(bins, nuis)),
        check_vma=False,
    )
```

```python
import jax
import jax.numpy as jnp
import numpy as np
from jax import lax
from jax.experimental import pallas as pl
from jax.experimental.pallas import tpu as pltpu
from jax.sharding import Mesh
from jax.sharding import PartitionSpec as P


F32 = jnp.float32
BF16 = jnp.bfloat16
SIDE = 4
PROC = 8
ROWS = 2048
BINS_DEV = 256
LANES = 128
CHUNKS = ROWS // LANES
PIECES = SIDE * SIDE
BIN_TOTAL = 32 * BINS_DEV
DEPTH = ROWS + BINS_DEV
VMEM = pl.BlockSpec(memory_space=pltpu.VMEM)
HBM = pl.BlockSpec(memory_space=pltpu.HBM)
SMEM = pl.BlockSpec(memory_space=pltpu.SMEM)
PARAMS = pltpu.CompilerParams(vmem_limit_bytes=12 * 1024 * 1024)


def cost(flops, moved):
    return pl.CostEstimate(flops=flops, bytes_accessed=moved, transcendentals=0)


def thirds(x):
    high = x.astype(BF16)
    rest = x - high.astype(F32)
    middle = rest.astype(BF16)
    low = (rest - middle.astype(F32)).astype(BF16)
    return [high, middle, low]


def rows_dot(a, b):
    return lax.dot_general(a, b, (((1,), (0,)), ((), ())), preferred_element_type=F32)


def packed(four):
    return jnp.concatenate(thirds(four) + [jnp.zeros((4, LANES), BF16)], 0)


def unpacked(rows):
    wide = rows.astype(F32)
    return wide[..., 0:4, :] + wide[..., 4:8, :] + wide[..., 8:12, :]


def project_kernel(v_ref, start_ref, dir_ref, out_ref, rows, flat, ends, sems):
    moves = [
        pltpu.make_async_copy(start_ref, ends.at[0:1], sems.at[0]),
        pltpu.make_async_copy(dir_ref, ends.at[1:2], sems.at[1]),
        pltpu.make_async_copy(v_ref, rows, sems.at[2]),
    ]
    for move in moves:
        move.start()
    for move in moves:
        move.wait()
    start, direction = ends[0:1, :], ends[1:2, :]
    parts = jnp.concatenate(thirds(start) + thirds(direction), 0)
    six = lax.dot_general(
        parts, rows[...], (((1,), (1,)), ((), ())), preferred_element_type=F32
    )
    along_start = six[0:1] + six[1:2] + six[2:3]
    along_dir = six[3:4] + six[4:5] + six[5:6]
    for c in range(CHUNKS):
        span = slice(c * LANES, (c + 1) * LANES)
        flat[c : c + 1, :] = along_start[:, span]
        flat[CHUNKS + c : CHUNKS + c + 1, :] = along_dir[:, span]
    tail = [start * direction, direction * direction, jnp.zeros((6, LANES), F32)]
    flat[2 * CHUNKS :, :] = jnp.concatenate(tail, 0)
    whole = flat[...]
    for i in range(out_ref.shape[0]):
        out_ref[i] = whole


def lane_groups_sum(x, lane):
    for k in (1, 2, 4):
        up = pltpu.roll(x, k, 1)
        down = pltpu.roll(x, LANES - k, 1)
        x = x + jnp.where((lane & k) != 0, up, down)
    return x


def layout_kernel(nominal_ref, counts_ref, steps_ref, out_ref):
    lane = lax.broadcasted_iota(jnp.int32, (CHUNKS, LANES), 1)
    place = lax.broadcasted_iota(jnp.int32, (CHUNKS, BINS_DEV), 1)
    line = lax.broadcasted_iota(jnp.int32, (CHUNKS, BINS_DEV), 0)
    mine = place // CHUNKS == line
    each = [nominal_ref[p : p + 1, :] for p in range(PROC)] + [counts_ref[...].astype(F32)]
    spread = jnp.concatenate([jnp.where(mine, row, 0.0) for row in each], 0)
    source = lax.broadcasted_iota(jnp.int32, (BINS_DEV, LANES), 0) % CHUNKS
    target = lax.broadcasted_iota(jnp.int32, (BINS_DEV, LANES), 1) // PROC
    pick = (source == target).astype(F32).astype(BF16)
    high, middle, low = (rows_dot(part, pick) for part in thirds(spread))
    moved = high + middle + low
    out = jnp.zeros((CHUNKS, LANES), F32)
    for p in range(PROC):
        out = jnp.where(lane % PROC == p, moved[p * CHUNKS : (p + 1) * CHUNKS], out)
    out_ref[0:CHUNKS, :] = out
    out_ref[CHUNKS : 2 * CHUNKS, :] = moved[PROC * CHUNKS :]
    for j in range(3):
        at = 2 * CHUNKS + j
        out_ref[at : at + 1, :] = jnp.full((1, LANES), steps_ref[j], F32)


def weights_kernel(got_ref, local_ref, w_ref, change_ref, sq_ref):
    total = jnp.sum(got_ref[...], axis=0)
    along_start = total[0:CHUNKS]
    along_dir = total[CHUNKS : 2 * CHUNKS]
    cross, square = total[2 * CHUNKS : 2 * CHUNKS + 1], total[2 * CHUNKS + 1 : 2 * CHUNKS + 2]
    lane = lax.broadcasted_iota(jnp.int32, (CHUNKS, LANES), 1)
    nominal, counts = local_ref[0:CHUNKS, :], local_ref[CHUNKS : 2 * CHUNKS, :]
    base = jnp.exp(nominal + along_start)
    base_total = lane_groups_sum(base, lane)
    base_log = jnp.log(base_total)
    part, norms = [], []
    for j in range(3):
        step = local_ref[2 * CHUNKS + j : 2 * CHUNKS + j + 1, :]
        shifted = jnp.exp(nominal + (along_start + step * along_dir))
        expected = lane_groups_sum(shifted, lane)
        change = (expected - base_total) - counts * (jnp.log(expected) - base_log)
        part.append(jnp.sum(change, axis=0, keepdims=True) * (1.0 / PROC))
        norms.append(step * (2.0 * cross + step * square))
    sq_ref[...] = jnp.concatenate(norms + [jnp.zeros((5, LANES), F32)], 0)
    residual = 1.0 - counts / base_total
    left = residual * base
    w_ref[0] = base
    w_ref[1] = left
    w_ref[2] = (counts / (base_total * base_total)) * base
    change_ref[...] = jnp.concatenate(part + [jnp.zeros((5, LANES), F32)], 0)


def bin_mask():
    mine = lax.broadcasted_iota(jnp.int32, (16, LANES), 1) // PROC
    return mine == lax.broadcasted_iota(jnp.int32, (16, LANES), 0)


def jacobian(weight, mine, blocks):
    spread = jnp.concatenate(thirds(jnp.where(mine, weight, 0.0)), 0)
    jac = rows_dot(spread, jnp.concatenate(blocks, 1))
    return (jac[0:16] + jac[16:32] + jac[32:48]).astype(BF16)


def product(pos_ref, right, blocks, jacs, first, kept_ref, sent_ref):
    px, py, core = pos_ref[0], pos_ref[1], pos_ref[4]
    steps = (0, 1 + 2 * core, 3 - 2 * core, 2)
    cols = [jnp.concatenate([b[...], jacs[:, k * LANES : (k + 1) * LANES]], 0) for k, b in enumerate(blocks)]
    term = rows_dot(right[...], jnp.concatenate(cols, 1))
    for i in range(SIDE):
        row_at = lax.rem(px + steps[i], SIDE)
        for half in range(2):
            part = term[i * LANES : (i + 1) * LANES, half * LANES : (half + 1) * LANES]
            upper, lower = part[0:64], part[64:]
            col_at = lax.rem(py + steps[first + half], SIDE)
            at = pl.ds(pl.multiple_of((row_at * SIDE + col_at) * 64, 64), 64)
            kept_ref[at, :] = jnp.where(core == 0, upper, lower)
            sent_ref[at, :] = jnp.where(core == 0, lower, upper).astype(BF16)


def rows_kernel(
    pos_ref, w_ref, change_ref, own, xa, xb, xr, ya, right, extra_ref, kept_ref, sent_ref,
    jac_rows, jac_cols, grad,
):
    mine = bin_mask()
    grad[...] = jnp.zeros((LANES, LANES), F32)

    def chunk(c, carry):
        span = pl.ds(pl.multiple_of(c * LANES, LANES), LANES)
        jac_span = pl.ds(pl.multiple_of(c * 16, 16), 16)
        base, left, curve = (w_ref[k, pl.ds(c, 1), :] for k in range(3))
        across = [ref[span, :] for ref in (own, xa, xb, xr)]
        jac_rows[jac_span, :] = jacobian(curve, mine, across)
        jac_cols[jac_span, :] = jacobian(base, mine, [ref[span, :] for ref in (own, ya)])
        for step, rows in enumerate(across):
            scaled = rows.T.astype(F32) * left
            if step == 0:
                grad[...] += scaled
            right[step * LANES : (step + 1) * LANES, span] = scaled.astype(BF16)
        return carry

    lax.fori_loop(0, CHUNKS, chunk, 0, unroll=4)
    right[:, ROWS:] = jac_rows[...].T
    total = jnp.sum(grad[...].T, axis=0, keepdims=True)
    extra = packed(jnp.concatenate([total, change_ref[0:3, :]], 0))
    extra_ref[...] = extra
    product(pos_ref, right, (own, ya), jac_cols, 0, kept_ref, sent_ref)
    sent_ref[PIECES * 64 :, :] = extra


def hessian_kernel(
    pos_ref, w_ref, right, yb, yr, kept_in, sent_in, kept_ref, sent_ref, jac_cols
):
    mine = bin_mask()
    for c in range(CHUNKS):
        rows = [ref[c * LANES : (c + 1) * LANES, :] for ref in (yb, yr)]
        jac_cols[c * 16 : (c + 1) * 16, :] = jacobian(w_ref[0, c : c + 1, :], mine, rows)
    product(pos_ref, right, (yb, yr), jac_cols, 2, kept_ref, sent_ref)


def pair_kernel(kept_ref, extra_ref, got_ref, out_ref):
    extra = packed(unpacked(extra_ref[...]) + unpacked(got_ref[PIECES * 64 :, :]))
    for k in range(PIECES):
        span = slice(k * 64, (k + 1) * 64)
        both = kept_ref[span, :] + got_ref[span, :].astype(F32)
        out_ref[k, 0:64, :] = both.astype(BF16)
        out_ref[k, 64:, :] = extra


def plane_kernel(pos_ref, got_ref, out_ref):
    py = pos_ref[1]
    extra = unpacked(got_ref[py, 64:, :])
    for k in range(1, SIDE):
        extra = extra + unpacked(got_ref[k * SIDE + py, 64:, :])
    extra = packed(extra)
    for j in range(SIDE):
        tile = got_ref[j, 0:64, :].astype(F32)
        for k in range(1, SIDE):
            tile = tile + got_ref[k * SIDE + j, 0:64, :].astype(F32)
        out_ref[j, 0:64, :] = tile.astype(BF16)
        out_ref[j, 64:, :] = extra


def finish_kernel(pos_ref, got_ref, sq_ref, start_ref, line_ref, grad_ref, hess_ref):
    scale = 1.0 / BIN_TOTAL
    tile = jnp.sum(got_ref[:, 0:64, :].astype(F32), axis=0)
    extra = jnp.sum(unpacked(got_ref[:, 64:, :]), axis=0)
    row = lax.broadcasted_iota(jnp.int32, (64, LANES), 0) + pos_ref[2] * 64
    col = lax.broadcasted_iota(jnp.int32, (64, LANES), 1) + pos_ref[3] * LANES
    hess_ref[...] = (tile + (row == col).astype(F32)) * scale
    grad_ref[...] = (extra[0:1] + start_ref[...]) * scale
    for j in range(3):
        line_ref[j] = jnp.sum(extra[1 + j : 2 + j, :] + 0.5 * sq_ref[j : j + 1, :]) * scale


def in_hbm(array):
    return pltpu.with_memory_space_constraint(array, pltpu.HBM)


def arrays_of(*shapes):
    return tuple(jax.ShapeDtypeStruct(s, d) for s, d in shapes)


def around(array, axis, way):
    pairs = []
    for core in range(2):
        step = way if core == 0 else -way
        pairs += [(core * SIDE + (i + step) % SIDE, core * SIDE + i) for i in range(SIDE)]
    return lax.ppermute(array, ("core", axis), pairs)


def exchanged(array, axes):
    return lax.all_to_all(array, axes, 0, 0, tiled=True)


def body(log_nominal, variations, observed, start, direction, step_lengths):
    own = variations.reshape(ROWS, LANES)
    sent, own = pl.pallas_call(
        project_kernel,
        out_shape=arrays_of(((16, 40, LANES), F32), ((ROWS, LANES), BF16)),
        in_specs=[HBM, HBM, HBM],
        out_specs=(VMEM, VMEM),
        scratch_shapes=[
            pltpu.VMEM((40, LANES), F32),
            pltpu.VMEM((8, LANES), F32),
            pltpu.SemaphoreType.DMA((3,)),
        ],
        compiler_params=PARAMS,
        cost_estimate=cost(10_000_000, 1_000_000),
        name="project",
    )(in_hbm(own), in_hbm(start[None, :]), in_hbm(direction[None, :]))
    xa, ya = (around(own, axis, 1) for axis in ("x", "y"))
    xb, yb = (around(own, axis, -1) for axis in ("x", "y"))
    xr, yr = (around(got, axis, 1) for got, axis in ((xa, "x"), (ya, "y")))
    got = exchanged(sent, ("y", "x"))
    local = pl.pallas_call(
        layout_kernel,
        out_shape=jax.ShapeDtypeStruct((40, LANES), F32),
        in_specs=[VMEM, VMEM, SMEM],
        out_specs=VMEM,
        compiler_params=PARAMS,
        cost_estimate=cost(10_000_000, 1_000_000),
        name="layout",
    )(*map(in_hbm, (log_nominal.T, observed[None, :], step_lengths)))
    weights, changes, squares = pl.pallas_call(
        weights_kernel,
        out_shape=arrays_of(
            ((3, CHUNKS, LANES), F32), ((8, LANES), F32), ((8, LANES), F32)
        ),
        in_specs=[VMEM, VMEM],
        out_specs=(VMEM, VMEM, VMEM),
        compiler_params=PARAMS,
        cost_estimate=cost(10_000_000, 1_000_000),
        name="weights",
    )(got, local)
    px, py = lax.axis_index("x"), lax.axis_index("y")
    core = lax.axis_index("core")
    block = lax.axis_index(("zh", "zl", "core"))
    position = jnp.stack([px, py, block, py * SIDE + px, core]).astype(jnp.int32)
    tiles = arrays_of(((PIECES * 64, LANES), F32), ((PIECES * 64 + 16, LANES), BF16))
    right, extra, kept, other = pl.pallas_call(
        rows_kernel,
        out_shape=arrays_of(((SIDE * LANES, DEPTH), BF16), ((16, LANES), BF16)) + tiles,
        in_specs=[SMEM] + [VMEM] * 7,
        out_specs=(VMEM, VMEM, VMEM, VMEM),
        scratch_shapes=[
            pltpu.VMEM((BINS_DEV, SIDE * LANES), BF16),
            pltpu.VMEM((BINS_DEV, 2 * LANES), BF16),
            pltpu.VMEM((LANES, LANES), F32),
        ],
        compiler_params=PARAMS,
        cost_estimate=cost(1_500_000_000, 5_000_000),
        name="rows",
    )(position, weights, changes, own, xa, xb, xr, ya)
    kept, other = pl.pallas_call(
        hessian_kernel,
        out_shape=tiles,
        in_specs=[SMEM] + [VMEM] * 6,
        out_specs=(VMEM, VMEM),
        scratch_shapes=[pltpu.VMEM((BINS_DEV, 2 * LANES), BF16)],
        input_output_aliases={5: 0, 6: 1},
        compiler_params=PARAMS,
        cost_estimate=cost(1_000_000_000, 5_000_000),
        name="hessian",
    )(position, weights, right, yb, yr, kept, other)
    swapped = lax.ppermute(other, "core", [(0, 1), (1, 0)])
    pair = pl.pallas_call(
        pair_kernel,
        out_shape=jax.ShapeDtypeStruct((PIECES, 80, LANES), BF16),
        in_specs=[VMEM] * 3,
        out_specs=VMEM,
        compiler_params=PARAMS,
        cost_estimate=cost(1_000_000, 1_000_000),
        name="pair",
    )(kept, extra, swapped)
    near = pl.pallas_call(
        plane_kernel,
        out_shape=jax.ShapeDtypeStruct((SIDE, 80, LANES), BF16),
        in_specs=[SMEM, VMEM],
        out_specs=VMEM,
        compiler_params=PARAMS,
        cost_estimate=cost(1_000_000, 1_000_000),
        name="plane",
    )(position, exchanged(pair, ("zl", "y")))
    line_change, gradient, hessian = pl.pallas_call(
        finish_kernel,
        out_shape=arrays_of(((3,), F32), ((1, LANES), F32), ((64, LANES), F32)),
        in_specs=[SMEM, VMEM, VMEM, VMEM],
        out_specs=(SMEM, VMEM, VMEM),
        compiler_params=PARAMS,
        cost_estimate=cost(1_000_000, 1_000_000),
        name="finish",
    )(position, exchanged(near, "zh"), squares, start[None, :])
    return line_change, gradient[0], hessian


def solution(mesh):
    split = Mesh(
        np.asarray(mesh.devices).reshape(SIDE, SIDE, 2, SIDE, SIDE),
        ("zh", "zl", "core", "y", "x"),
    )
    bins, nuis = ("zh", "zl", "core"), ("y", "x")
    placed = (P(bins, None), P(bins, None, nuis), P(bins), P(nuis), P(nuis), P())
    return jax.shard_map(
        body,
        mesh=split,
        in_specs=placed,
        out_specs=(P(), P(nuis), P(bins, nuis)),
        check_vma=False,
    )
```

```python
import jax
import jax.numpy as jnp
import numpy as np
from jax import lax
from jax.experimental import pallas as pl
from jax.experimental.pallas import tpu as pltpu
from jax.sharding import Mesh
from jax.sharding import PartitionSpec as P


F32 = jnp.float32
BF16 = jnp.bfloat16
SIDE = 4
PROC = 8
ROWS = 2048
BINS_DEV = 256
LANES = 128
CHUNKS = ROWS // LANES
PIECES = SIDE * SIDE
BIN_TOTAL = 32 * BINS_DEV
DEPTH = ROWS + BINS_DEV
VMEM = pl.BlockSpec(memory_space=pltpu.VMEM)
HBM = pl.BlockSpec(memory_space=pltpu.HBM)
SMEM = pl.BlockSpec(memory_space=pltpu.SMEM)
PARAMS = pltpu.CompilerParams(vmem_limit_bytes=12 * 1024 * 1024)


def cost(flops, moved):
    return pl.CostEstimate(flops=flops, bytes_accessed=moved, transcendentals=0)


def thirds(x):
    high = x.astype(BF16)
    rest = x - high.astype(F32)
    middle = rest.astype(BF16)
    low = (rest - middle.astype(F32)).astype(BF16)
    return [high, middle, low]


def rows_dot(a, b):
    return lax.dot_general(a, b, (((1,), (0,)), ((), ())), preferred_element_type=F32)


def packed(two):
    return jnp.concatenate(thirds(two) + [jnp.zeros((2, LANES), BF16)], 0)


def unpacked(rows):
    wide = rows.astype(F32)
    return wide[..., 0:2, :] + wide[..., 2:4, :] + wide[..., 4:6, :]


def in_lanes(parts):
    lane = lax.broadcasted_iota(jnp.int32, (1, LANES), 1)
    row = jnp.zeros((1, LANES), F32)
    for j, part in enumerate(parts):
        row = jnp.where(lane == j, jnp.sum(part, axis=1, keepdims=True), row)
    return jnp.concatenate([row, jnp.zeros((7, LANES), F32)], 0)


def project_kernel(v_ref, start_ref, dir_ref, out_ref, rows, flat, ends, sems):
    moves = [
        pltpu.make_async_copy(start_ref, ends.at[0:1], sems.at[0]),
        pltpu.make_async_copy(dir_ref, ends.at[1:2], sems.at[1]),
        pltpu.make_async_copy(v_ref, rows, sems.at[2]),
    ]
    for move in moves:
        move.start()
    for move in moves:
        move.wait()
    start, direction = ends[0:1, :], ends[1:2, :]
    parts = jnp.concatenate(thirds(start) + thirds(direction), 0)
    six = lax.dot_general(
        parts, rows[...], (((1,), (1,)), ((), ())), preferred_element_type=F32
    )
    along_start = six[0:1] + six[1:2] + six[2:3]
    along_dir = six[3:4] + six[4:5] + six[5:6]
    for c in range(CHUNKS):
        span = slice(c * LANES, (c + 1) * LANES)
        flat[c : c + 1, :] = along_start[:, span]
        flat[CHUNKS + c : CHUNKS + c + 1, :] = along_dir[:, span]
    tail = [start * direction, direction * direction, jnp.zeros((6, LANES), F32)]
    flat[2 * CHUNKS :, :] = jnp.concatenate(tail, 0)
    whole = flat[...]
    for i in range(out_ref.shape[0]):
        out_ref[i] = whole


def lane_groups_sum(x, lane):
    for k in (1, 2, 4):
        up = pltpu.roll(x, k, 1)
        down = pltpu.roll(x, LANES - k, 1)
        x = x + jnp.where((lane & k) != 0, up, down)
    return x


def layout_kernel(nominal_ref, counts_ref, steps_ref, out_ref):
    lane = lax.broadcasted_iota(jnp.int32, (CHUNKS, LANES), 1)
    place = lax.broadcasted_iota(jnp.int32, (CHUNKS, BINS_DEV), 1)
    line = lax.broadcasted_iota(jnp.int32, (CHUNKS, BINS_DEV), 0)
    mine = place // CHUNKS == line
    each = [nominal_ref[p : p + 1, :] for p in range(PROC)] + [counts_ref[...].astype(F32)]
    spread = jnp.concatenate([jnp.where(mine, row, 0.0) for row in each], 0)
    source = lax.broadcasted_iota(jnp.int32, (BINS_DEV, LANES), 0) % CHUNKS
    target = lax.broadcasted_iota(jnp.int32, (BINS_DEV, LANES), 1) // PROC
    pick = (source == target).astype(F32).astype(BF16)
    high, middle, low = (rows_dot(part, pick) for part in thirds(spread))
    moved = high + middle + low
    out = jnp.zeros((CHUNKS, LANES), F32)
    for p in range(PROC):
        out = jnp.where(lane % PROC == p, moved[p * CHUNKS : (p + 1) * CHUNKS], out)
    out_ref[0:CHUNKS, :] = out
    out_ref[CHUNKS : 2 * CHUNKS, :] = moved[PROC * CHUNKS :]
    for j in range(3):
        at = 2 * CHUNKS + j
        out_ref[at : at + 1, :] = jnp.full((1, LANES), steps_ref[j], F32)


def weights_kernel(got_ref, local_ref, w_ref, change_ref, sq_ref):
    total = jnp.sum(got_ref[...], axis=0)
    along_start = total[0:CHUNKS]
    along_dir = total[CHUNKS : 2 * CHUNKS]
    cross, square = total[2 * CHUNKS : 2 * CHUNKS + 1], total[2 * CHUNKS + 1 : 2 * CHUNKS + 2]
    lane = lax.broadcasted_iota(jnp.int32, (CHUNKS, LANES), 1)
    nominal, counts = local_ref[0:CHUNKS, :], local_ref[CHUNKS : 2 * CHUNKS, :]
    base = jnp.exp(nominal + along_start)
    base_total = lane_groups_sum(base, lane)
    base_log = jnp.log(base_total)
    part, norms = [], []
    for j in range(3):
        step = local_ref[2 * CHUNKS + j : 2 * CHUNKS + j + 1, :]
        shifted = jnp.exp(nominal + (along_start + step * along_dir))
        expected = lane_groups_sum(shifted, lane)
        change = (expected - base_total) - counts * (jnp.log(expected) - base_log)
        part.append(jnp.sum(change, axis=0, keepdims=True) * (1.0 / PROC))
        norms.append(step * (2.0 * cross + step * square))
    sq_ref[...] = in_lanes(norms)
    residual = 1.0 - counts / base_total
    left = residual * base
    w_ref[0] = base
    w_ref[1] = left
    w_ref[2] = (counts / (base_total * base_total)) * base
    change_ref[...] = in_lanes(part)


def bin_mask():
    mine = lax.broadcasted_iota(jnp.int32, (16, LANES), 1) // PROC
    return mine == lax.broadcasted_iota(jnp.int32, (16, LANES), 0)


def jacobian(weight, mine, blocks):
    spread = jnp.concatenate(thirds(jnp.where(mine, weight, 0.0)), 0)
    jac = rows_dot(spread, jnp.concatenate(blocks, 1))
    return (jac[0:16] + jac[16:32] + jac[32:48]).astype(BF16)


def product(pos_ref, right, blocks, jacs, first, kept_ref, sent_ref):
    px, py, core = pos_ref[0], pos_ref[1], pos_ref[4]
    steps = (0, 1 + 2 * core, 3 - 2 * core, 2)
    cols = [jnp.concatenate([b[...], jacs[:, k * LANES : (k + 1) * LANES]], 0) for k, b in enumerate(blocks)]
    term = rows_dot(right[...], jnp.concatenate(cols, 1))
    for i in range(SIDE):
        row_at = lax.rem(px + steps[i], SIDE)
        for half in range(2):
            part = term[i * LANES : (i + 1) * LANES, half * LANES : (half + 1) * LANES]
            upper, lower = part[0:64], part[64:]
            col_at = lax.rem(py + steps[first + half], SIDE)
            at = pl.ds(pl.multiple_of((row_at * SIDE + col_at) * 64, 64), 64)
            kept_ref[at, :] = jnp.where(core == 0, upper, lower)
            sent_ref[at, :] = jnp.where(core == 0, lower, upper).astype(BF16)


def rows_kernel(
    pos_ref, w_ref, change_ref, own, xa, xb, xr, ya, right, extra_ref, kept_ref, sent_ref,
    jac_rows, jac_cols, grad,
):
    mine = bin_mask()
    grad[...] = jnp.zeros((LANES, LANES), F32)

    def chunk(c, carry):
        span = pl.ds(pl.multiple_of(c * LANES, LANES), LANES)
        jac_span = pl.ds(pl.multiple_of(c * 16, 16), 16)
        base, left, curve = (w_ref[k, pl.ds(c, 1), :] for k in range(3))
        across = [ref[span, :] for ref in (own, xa, xb, xr)]
        jac_rows[jac_span, :] = jacobian(curve, mine, across)
        jac_cols[jac_span, :] = jacobian(base, mine, [ref[span, :] for ref in (own, ya)])
        for step, rows in enumerate(across):
            scaled = rows.T.astype(F32) * left
            if step == 0:
                grad[...] += scaled
            right[step * LANES : (step + 1) * LANES, span] = scaled.astype(BF16)
        return carry

    lax.fori_loop(0, CHUNKS, chunk, 0, unroll=4)
    right[:, ROWS:] = jac_rows[...].T
    total = jnp.sum(grad[...].T, axis=0, keepdims=True)
    extra = packed(jnp.concatenate([total, change_ref[0:1, :]], 0))
    extra_ref[...] = extra
    product(pos_ref, right, (own, ya), jac_cols, 0, kept_ref, sent_ref)
    sent_ref[PIECES * 64 :, :] = extra


def hessian_kernel(
    pos_ref, w_ref, right, yb, yr, kept_in, sent_in, kept_ref, sent_ref, jac_cols
):
    mine = bin_mask()
    for c in range(CHUNKS):
        rows = [ref[c * LANES : (c + 1) * LANES, :] for ref in (yb, yr)]
        jac_cols[c * 16 : (c + 1) * 16, :] = jacobian(w_ref[0, c : c + 1, :], mine, rows)
    product(pos_ref, right, (yb, yr), jac_cols, 2, kept_ref, sent_ref)


def pair_kernel(kept_ref, extra_ref, got_ref, out_ref):
    extra = packed(unpacked(extra_ref[...]) + unpacked(got_ref[PIECES * 64 :, :]))
    for k in range(PIECES):
        span = slice(k * 64, (k + 1) * 64)
        both = kept_ref[span, :] + got_ref[span, :].astype(F32)
        out_ref[k, 0:64, :] = both.astype(BF16)
        out_ref[k, 64:, :] = extra


def plane_kernel(pos_ref, got_ref, out_ref):
    py = pos_ref[1]
    extra = unpacked(got_ref[py, 64:, :])
    for k in range(1, SIDE):
        extra = extra + unpacked(got_ref[k * SIDE + py, 64:, :])
    extra = packed(extra)
    for j in range(SIDE):
        tile = got_ref[j, 0:64, :].astype(F32)
        for k in range(1, SIDE):
            tile = tile + got_ref[k * SIDE + j, 0:64, :].astype(F32)
        out_ref[j, 0:64, :] = tile.astype(BF16)
        out_ref[j, 64:, :] = extra


def finish_kernel(pos_ref, got_ref, sq_ref, start_ref, line_ref, grad_ref, hess_ref):
    scale = 1.0 / BIN_TOTAL
    tile = jnp.sum(got_ref[:, 0:64, :].astype(F32), axis=0)
    extra = jnp.sum(unpacked(got_ref[:, 64:, :]), axis=0)
    row = lax.broadcasted_iota(jnp.int32, (64, LANES), 0) + pos_ref[2] * 64
    col = lax.broadcasted_iota(jnp.int32, (64, LANES), 1) + pos_ref[3] * LANES
    hess_ref[...] = (tile + (row == col).astype(F32)) * scale
    grad_ref[...] = (extra[0:1] + start_ref[...]) * scale
    line = (extra[1:2] + 0.5 * sq_ref[0:1, :]) * scale
    for j in range(3):
        line_ref[j] = line[0, j]


def in_hbm(array):
    return pltpu.with_memory_space_constraint(array, pltpu.HBM)


def arrays_of(*shapes):
    return tuple(jax.ShapeDtypeStruct(s, d) for s, d in shapes)


def around(array, axis, way):
    pairs = []
    for core in range(2):
        step = way if core == 0 else -way
        pairs += [(core * SIDE + (i + step) % SIDE, core * SIDE + i) for i in range(SIDE)]
    return lax.ppermute(array, ("core", axis), pairs)


def exchanged(array, axes):
    return lax.all_to_all(array, axes, 0, 0, tiled=True)


def body(log_nominal, variations, observed, start, direction, step_lengths):
    own = variations.reshape(ROWS, LANES)
    sent, own = pl.pallas_call(
        project_kernel,
        out_shape=arrays_of(((16, 40, LANES), F32), ((ROWS, LANES), BF16)),
        in_specs=[HBM, HBM, HBM],
        out_specs=(VMEM, VMEM),
        scratch_shapes=[
            pltpu.VMEM((40, LANES), F32),
            pltpu.VMEM((8, LANES), F32),
            pltpu.SemaphoreType.DMA((3,)),
        ],
        compiler_params=PARAMS,
        cost_estimate=cost(10_000_000, 1_000_000),
        name="project",
    )(in_hbm(own), in_hbm(start[None, :]), in_hbm(direction[None, :]))
    xa, ya = (around(own, axis, 1) for axis in ("x", "y"))
    xb, yb = (around(own, axis, -1) for axis in ("x", "y"))
    xr, yr = (around(got, axis, 1) for got, axis in ((xa, "x"), (ya, "y")))
    got = exchanged(sent, ("y", "x"))
    local = pl.pallas_call(
        layout_kernel,
        out_shape=jax.ShapeDtypeStruct((40, LANES), F32),
        in_specs=[VMEM, VMEM, SMEM],
        out_specs=VMEM,
        compiler_params=PARAMS,
        cost_estimate=cost(10_000_000, 1_000_000),
        name="layout",
    )(*map(in_hbm, (log_nominal.T, observed[None, :], step_lengths)))
    weights, changes, squares = pl.pallas_call(
        weights_kernel,
        out_shape=arrays_of(
            ((3, CHUNKS, LANES), F32), ((8, LANES), F32), ((8, LANES), F32)
        ),
        in_specs=[VMEM, VMEM],
        out_specs=(VMEM, VMEM, VMEM),
        compiler_params=PARAMS,
        cost_estimate=cost(10_000_000, 1_000_000),
        name="weights",
    )(got, local)
    px, py = lax.axis_index("x"), lax.axis_index("y")
    core = lax.axis_index("core")
    block = lax.axis_index(("zh", "zl", "core"))
    position = jnp.stack([px, py, block, py * SIDE + px, core]).astype(jnp.int32)
    tiles = arrays_of(((PIECES * 64, LANES), F32), ((PIECES * 64 + 8, LANES), BF16))
    right, extra, kept, other = pl.pallas_call(
        rows_kernel,
        out_shape=arrays_of(((SIDE * LANES, DEPTH), BF16), ((8, LANES), BF16)) + tiles,
        in_specs=[SMEM] + [VMEM] * 7,
        out_specs=(VMEM, VMEM, VMEM, VMEM),
        scratch_shapes=[
            pltpu.VMEM((BINS_DEV, SIDE * LANES), BF16),
            pltpu.VMEM((BINS_DEV, 2 * LANES), BF16),
            pltpu.VMEM((LANES, LANES), F32),
        ],
        compiler_params=PARAMS,
        cost_estimate=cost(1_500_000_000, 5_000_000),
        name="rows",
    )(position, weights, changes, own, xa, xb, xr, ya)
    kept, other = pl.pallas_call(
        hessian_kernel,
        out_shape=tiles,
        in_specs=[SMEM] + [VMEM] * 6,
        out_specs=(VMEM, VMEM),
        scratch_shapes=[pltpu.VMEM((BINS_DEV, 2 * LANES), BF16)],
        input_output_aliases={5: 0, 6: 1},
        compiler_params=PARAMS,
        cost_estimate=cost(1_000_000_000, 5_000_000),
        name="hessian",
    )(position, weights, right, yb, yr, kept, other)
    swapped = lax.ppermute(other, "core", [(0, 1), (1, 0)])
    pair = pl.pallas_call(
        pair_kernel,
        out_shape=jax.ShapeDtypeStruct((PIECES, 72, LANES), BF16),
        in_specs=[VMEM] * 3,
        out_specs=VMEM,
        compiler_params=PARAMS,
        cost_estimate=cost(1_000_000, 1_000_000),
        name="pair",
    )(kept, extra, swapped)
    near = pl.pallas_call(
        plane_kernel,
        out_shape=jax.ShapeDtypeStruct((SIDE, 72, LANES), BF16),
        in_specs=[SMEM, VMEM],
        out_specs=VMEM,
        compiler_params=PARAMS,
        cost_estimate=cost(1_000_000, 1_000_000),
        name="plane",
    )(position, exchanged(pair, ("zl", "y")))
    line_change, gradient, hessian = pl.pallas_call(
        finish_kernel,
        out_shape=arrays_of(((3,), F32), ((1, LANES), F32), ((64, LANES), F32)),
        in_specs=[SMEM, VMEM, VMEM, VMEM],
        out_specs=(SMEM, VMEM, VMEM),
        compiler_params=PARAMS,
        cost_estimate=cost(1_000_000, 1_000_000),
        name="finish",
    )(position, exchanged(near, "zh"), squares, start[None, :])
    return line_change, gradient[0], hessian


def solution(mesh):
    split = Mesh(
        np.asarray(mesh.devices).reshape(SIDE, SIDE, 2, SIDE, SIDE),
        ("zh", "zl", "core", "y", "x"),
    )
    bins, nuis = ("zh", "zl", "core"), ("y", "x")
    placed = (P(bins, None), P(bins, None, nuis), P(bins), P(nuis), P(nuis), P())
    return jax.shard_map(
        body,
        mesh=split,
        in_specs=placed,
        out_specs=(P(), P(nuis), P(bins, nuis)),
        check_vma=False,
    )
```
